256 devices in a mesh: region: 8 (over z), owner: 32 (over x, y, core).
Axes of the slice: x: 4, y: 4, z: 8, core: 2. Of those that a mesh axis runs over, the one named last changes fastest.
Arguments:
- features: bfloat16 [1024, 64, 1728], P(('region', 'owner')), may hold values from -6 to 6
- conv_weight: bfloat16 [27, 64, 64], replicated, may hold values from -0.15625 to 0.15625
- down_weight: bfloat16 [8, 128, 64], replicated, may hold values from -0.25 to 0.25
- fine_grad: bfloat16 [1024, 64, 1728], P(('region', 'owner')), may hold values from -6 to 6
- coarse_grad: bfloat16 [256, 128, 8, 216], P(('region', 'owner')), may hold values from -6 to 6
- face_send: int32 [256, 2, 4, 2], P(('region', 'owner')), may hold values from 0 to 7, as said below
- face_recv: int32 [1024, 2, 2], P(('region', 'owner')), may hold values from 8 to 15, as said below
- z_recv: int32 [1024, 2], P(('region', 'owner')), may hold values from 0 to 8, as said below
- parent_send: int32 [256, 4], P(('region', 'owner')), may hold values from 0 to 3, as said below
- parent_recv: int32 [256, 8], P(('region', 'owner')), may hold values from 0 to 4, as said below
Outputs:
- fine_out: bfloat16 [1024, 64, 1728], P(('region', 'owner'))
- coarse_out: bfloat16 [256, 128, 8, 216], P(('region', 'owner'))
- grad_in: bfloat16 [1024, 64, 1728], P(('region', 'owner'))
- grad_conv: float32 [27, 64, 64], replicated
- grad_down: float32 [8, 128, 64], replicated
The draws below stay inside these ranges and needn't reach their ends.
Inputs may be any that keep to these rules, and one draw needn't show every extreme that they name: `face_send`: entry [d, m, s] names one of the device's own faces of round d; each of its 8 faces is named exactly once in each round. `face_recv`: every entry names a received face. `z_recv`: 8 names the zero face; the lowest region's entry 0 and the highest region's entry 1 are always it. `parent_send`: each row is a permutation of the device's slots. `parent_recv`: entry q is a distance index or 4 for an empty octant; each distance index is named exactly once in a row.
All inputs are finite; a program needn't handle non-finite values.
Results may differ from the reference program's by a relative error of at most 0.005.
Values may be sent and summed in bfloat16 or wider, within the bound.
A program may use at most 64 MiB of HBM per device.

```python
import math
import jax
import jax.numpy as jnp
from jax import lax

C = 64
C2 = 128
EDGE = 12
BRICK_DEV = 4
PCAP = 2
VOX = 1728
BRICKS = 1024
PARENTS = 256
N_REGION = 8
N_OWNER = 32


OFFSETS = (1, -1, 2, -2)


SLOT_PAIRS = (((0, 1), (2, 3)), ((2, 3), (0, 1)))


def lateral_bits(key):
    return jax.random.randint(jax.random.fold_in(key, 11), (N_REGION, N_OWNER, 2, 4), 0, 2).astype(jnp.int32)


def draw_face_send(key, part):
    flip_bits = lateral_bits(key)
    rounds = []
    for round_index in range(2):
        columns = []
        for index, shift_by in enumerate(OFFSETS):
            first_slot = SLOT_PAIRS[round_index][abs(shift_by) - 1][0]
            base = BRICK_DEV if shift_by > 0 else 0
            bit = flip_bits[:, :, round_index, index]
            positions = [base + first_slot + (place + bit) % 2 for place in range(PCAP)]
            columns.append(jnp.stack(positions, axis=-1))
        rounds.append(jnp.stack(columns, axis=2))
    index_table = jnp.stack(rounds, axis=2)
    return index_table.reshape(N_REGION * N_OWNER, 2, 4, PCAP).astype(jnp.int32)


def draw_face_recv(key, part):
    flip_bits = lateral_bits(key)
    owner_ids = jnp.arange(N_OWNER, dtype=jnp.int32)
    rounds = []
    for round_index in range(2):
        slots = []
        for slot in range(BRICK_DEV):
            distance = 1 if slot in SLOT_PAIRS[round_index][0] else 2
            up_index = OFFSETS.index(distance)
            down_index = OFFSETS.index(-distance)
            lower_owner = (owner_ids - distance) % N_OWNER
            upper_owner = (owner_ids + distance) % N_OWNER
            low_bit = flip_bits[:, lower_owner, round_index, up_index]
            high_bit = flip_bits[:, upper_owner, round_index, down_index]
            low_source = 2 * BRICK_DEV + up_index * PCAP + (slot % 2 + low_bit) % 2
            high_source = 2 * BRICK_DEV + down_index * PCAP + (slot % 2 + high_bit) % 2
            slots.append(jnp.stack([low_source, high_source], axis=-1))
        rounds.append(jnp.stack(slots, axis=2))
    index_table = jnp.stack(rounds, axis=3)
    return index_table.reshape(N_REGION * N_OWNER * BRICK_DEV, 2, 2).astype(jnp.int32)


def draw_z_recv(key, part):
    brick_slots = BRICK_DEV
    flip_bits = jax.random.randint(jax.random.fold_in(key, 12), (N_REGION, 2), 0, 2).astype(jnp.int32)
    slot_ids = jnp.arange(brick_slots, dtype=jnp.int32)
    slot_group = slot_ids // 2
    parity = slot_ids % 2
    partner = slot_ids[None, :] + flip_bits[:, slot_group] * (1 - 2 * parity[None, :])
    region_ids = jnp.arange(N_REGION, dtype=jnp.int32)[:, None]
    below_partner = jnp.concatenate([partner[:1], partner[:-1]], axis=0)
    low_entry = jnp.where(region_ids > 0, below_partner, 2 * brick_slots)
    high_entry = jnp.where(region_ids < N_REGION - 1, brick_slots + partner, 2 * brick_slots)
    both_entries = jnp.stack([low_entry, high_entry], axis=-1)
    index_table = jnp.broadcast_to(both_entries[:, None], (N_REGION, N_OWNER, brick_slots, 2))
    return index_table.reshape(N_REGION * N_OWNER * brick_slots, 2).astype(jnp.int32)


def draw_parent_send(key, part):
    device_keys = jax.vmap(lambda index: jax.random.fold_in(key, 400 + index))(jnp.arange(N_REGION * N_OWNER))
    orders = jax.vmap(lambda device_key: jax.random.permutation(device_key, BRICK_DEV))(device_keys)
    return orders.astype(jnp.int32)


def draw_parent_recv(key, part):
    device_keys = jax.vmap(lambda index: jax.random.fold_in(key, 900 + index))(jnp.arange(N_REGION * N_OWNER))
    octant_order = jax.vmap(lambda device_key: jax.random.permutation(device_key, 8))(device_keys).astype(jnp.int32)
    device_ids = jnp.arange(N_REGION * N_OWNER, dtype=jnp.int32)
    index_table = jnp.full((N_REGION * N_OWNER, 8), BRICK_DEV, jnp.int32)
    for index in range(4):
        index_table = index_table.at[device_ids, octant_order[:, index]].set(index)
    return index_table


def shard_levels(own_key, dims, split, smallest, largest):
    factor_of = 1.0
    for position, parts in split:
        heights = jax.random.uniform(jax.random.fold_in(jax.random.fold_in(own_key, 6), position), (parts,), jnp.float32, smallest / len(split), largest / len(split))
        factor_of = factor_of * jnp.repeat(jnp.exp(heights), dims[position] // parts).reshape((-1,) + (1,) * (len(dims) - 1 - position))
    return factor_of


def gaussian(key, shape, deviation, most, cuts=(), kind=jnp.bfloat16):
    array = deviation * jax.random.normal(key, shape, jnp.float32)
    if cuts:
        array = array * shard_levels(key, shape, cuts, -0.22, 0.18)
    return jnp.clip(array, -most, most).astype(kind)


def setup_inputs(seed: int = 0) -> dict:
    splits = jax.random.split(jax.random.key(seed), 11)
    return {
        "features": gaussian(splits[0], (BRICKS, C, VOX), 1.0, 6.0, ((0, 256),)),
        "conv_weight": gaussian(splits[1], (27, C, C), (27 * C) ** -0.5, 0.15625),
        "down_weight": gaussian(splits[2], (8, C2, C), (8 * C) ** -0.5, 0.25),
        "fine_grad": gaussian(splits[3], (BRICKS, C, VOX), 1.0, 6.0, ((0, 256),)),
        "coarse_grad": gaussian(splits[4], (PARENTS, C2, 8, VOX // 8), 1.0, 6.0, ((0, 256),)),
        "face_send": draw_face_send(jax.random.fold_in(splits[10], 71), 0),
        "face_recv": draw_face_recv(jax.random.fold_in(splits[10], 71), 0),
        "z_recv": draw_z_recv(jax.random.fold_in(splits[10], 71), 0),
        "parent_send": draw_parent_send(jax.random.fold_in(splits[10], 71), 0),
        "parent_recv": draw_parent_recv(jax.random.fold_in(splits[10], 71), 0),
    }


OFFSETS = (1, -1, 2, -2)

def pick_rows(table_rows, chosen_rows):
    return jax.vmap(lambda source, selector: source[selector])(table_rows, chosen_rows)

def face_pair(volume, face_axis):
    low_face = lax.index_in_dim(volume, 0, face_axis, keepdims=False)
    high_face = lax.index_in_dim(volume, volume.shape[face_axis] - 1, face_axis, keepdims=False)
    return (low_face, high_face)

def owner_round(volume, face_axis, send_list, recv_list):
    low_face, high_face = face_pair(volume, face_axis)
    face_pool = jnp.concatenate([low_face, high_face], axis=1)
    outgoing = pick_rows(face_pool, send_list)
    incoming = jnp.stack([jnp.roll(outgoing[:, index], shift_by, axis=0) for index, shift_by in enumerate(OFFSETS)], axis=1)
    incoming = incoming.reshape((incoming.shape[0], -1) + incoming.shape[3:])
    all_faces = jnp.concatenate([face_pool, incoming], axis=1)
    low_pad = pick_rows(all_faces, recv_list[..., 0])
    high_pad = pick_rows(all_faces, recv_list[..., 1])
    return jnp.concatenate([jnp.expand_dims(low_pad, face_axis), volume, jnp.expand_dims(high_pad, face_axis)], axis=face_axis)

def slab_round(volume, z_list):
    low_face, high_face = face_pair(volume, 6)
    zero_layer = jnp.zeros_like(low_face[:1])
    from_below = jnp.concatenate([zero_layer, high_face[:-1]], axis=0)
    from_above = jnp.concatenate([low_face[1:], zero_layer], axis=0)
    face_pool = jnp.concatenate([from_below, from_above, jnp.zeros_like(low_face[:, :, :1])], axis=2)
    low_pad = jax.vmap(pick_rows)(face_pool, z_list[..., 0])
    high_pad = jax.vmap(pick_rows)(face_pool, z_list[..., 1])
    return jnp.concatenate([low_pad[..., None], volume, high_pad[..., None]], axis=6)

def pad_all(volume, send_grid, recv_grid, z_grid):

    def lateral(region_items):
        region_volume, send_list, recv_list = region_items
        region_volume = owner_round(region_volume, 3, send_list[:, 0], recv_list[:, :, 0])
        return owner_round(region_volume, 4, send_list[:, 1], recv_list[:, :, 1])
    volume = lax.map(lateral, (volume, send_grid, recv_grid))
    return slab_round(volume, z_grid)

def conv_valid(operand, kernel, numbers):
    return lax.conv_general_dilated(operand.astype(jnp.float32), kernel.astype(jnp.float32), (1, 1, 1), 'VALID', dimension_numbers=numbers, precision=lax.Precision.HIGHEST)

def to_taps(volume):
    bricks, channels = volume.shape[:2]
    half_edge = EDGE // 2
    blocks = volume.reshape(bricks, channels, half_edge, 2, half_edge, 2, half_edge, 2)
    return blocks.transpose(0, 3, 5, 7, 1, 2, 4, 6).reshape(bricks, 8 * channels, half_edge ** 3)

def from_taps(stacked, channels):
    bricks = stacked.shape[0]
    half_edge = EDGE // 2
    blocks = stacked.reshape(bricks, 2, 2, 2, channels, half_edge, half_edge, half_edge)
    return blocks.transpose(0, 4, 5, 1, 6, 2, 7, 3).reshape(bricks, channels, EDGE, EDGE, EDGE)

def coarse_region(region_items):
    contributions, send_list, recv_list = region_items
    outgoing = pick_rows(contributions, send_list)
    received = jnp.stack([jnp.roll(outgoing[:, index], index + 1, axis=0) for index in range(4)], axis=1)
    received = jnp.concatenate([received, jnp.zeros_like(received[:, :1])], axis=1)
    return pick_rows(received, recv_list)

def child_region(region_items):
    octant_grad, send_list, recv_list = region_items
    octant_hits = (recv_list[:, None, :] == jnp.arange(4)[None, :, None]).astype(jnp.float32)
    returning = jnp.einsum('pmq,pqcu->pmcu', octant_hits, octant_grad.astype(jnp.float32), precision=lax.Precision.HIGHEST)
    arrived = jnp.stack([jnp.roll(returning[:, index], -(index + 1), axis=0) for index in range(4)], axis=1)
    slot_hits = (send_list[:, :, None] == jnp.arange(BRICK_DEV)[None, None, :]).astype(jnp.float32)
    return jnp.einsum('omk,omcu->okcu', slot_hits, arrived, precision=lax.Precision.HIGHEST).astype(jnp.bfloat16)

def reference(features, conv_weight, down_weight, fine_grad, coarse_grad, face_send, face_recv, z_recv, parent_send, parent_recv):
    regions = N_REGION
    owners = N_OWNER
    brick_slots = BRICK_DEV
    pad_edge = EDGE + 2
    octant_vox = VOX // 8
    send_grid = face_send.reshape(regions, owners, 2, 4, PCAP)
    recv_grid = face_recv.reshape(regions, owners, brick_slots, 2, 2)
    z_grid = z_recv.reshape(regions, owners, brick_slots, 2)
    volume_shape = (regions, owners, brick_slots, C, EDGE, EDGE, EDGE)
    block_shape = (regions, owners * brick_slots, C, pad_edge, pad_edge, pad_edge)
    padded = pad_all(features.reshape(volume_shape), send_grid, recv_grid, z_grid)
    padded_blocks = padded.reshape(block_shape)
    kernel = conv_weight.reshape(3, 3, 3, C, C).transpose(3, 4, 0, 1, 2)
    forward_numbers = ('NCDHW', 'OIDHW', 'NCDHW')
    pre_act = lax.map(lambda region_block: conv_valid(region_block, kernel, forward_numbers), padded_blocks)
    pre_act = pre_act.reshape(BRICKS, C, EDGE, EDGE, EDGE)
    fine_out = jax.nn.silu(pre_act).astype(jnp.bfloat16)
    down_matrix = down_weight.transpose(1, 0, 2).reshape(C2, 8 * C).astype(jnp.float32)

    def contribute(region_fine):
        octant_taps = to_taps(region_fine).astype(jnp.float32)
        return jnp.einsum('ok,bkl->bol', down_matrix, octant_taps, precision=lax.Precision.HIGHEST).astype(jnp.bfloat16)
    contributions = lax.map(contribute, fine_out.reshape(regions, owners * brick_slots, C, EDGE, EDGE, EDGE))
    contributions = contributions.reshape(regions, owners, brick_slots, C2, octant_vox)
    send_parent = parent_send.reshape(regions, owners, 4)
    recv_parent = parent_recv.reshape(regions, owners, 8)
    coarse_out = lax.map(coarse_region, (contributions, send_parent, recv_parent))
    coarse_out = coarse_out.transpose(0, 1, 3, 2, 4).reshape(PARENTS, C2, 8, octant_vox)
    octant_grad = coarse_grad.reshape(regions, owners, C2, 8, octant_vox).transpose(0, 1, 3, 2, 4)
    child_grad = lax.map(child_region, (octant_grad, send_parent, recv_parent))
    child_grad = child_grad.reshape(regions, owners * brick_slots, C2, octant_vox)

    def coarse_grads(region_items):
        region_child, region_fine = region_items
        child_float = region_child.astype(jnp.float32)
        stacked = jnp.einsum('ok,bol->bkl', down_matrix, child_float, precision=lax.Precision.HIGHEST)
        taps_float = to_taps(region_fine).astype(jnp.float32)
        down_terms = jnp.einsum('bol,bkl->ok', child_float, taps_float, precision=lax.Precision.HIGHEST)
        return (from_taps(stacked, C), down_terms)
    up_grad, down_terms = lax.map(coarse_grads, (child_grad, fine_out.reshape(regions, owners * brick_slots, C, EDGE, EDGE, EDGE)))
    up_grad = up_grad.reshape(BRICKS, C, EDGE, EDGE, EDGE)
    sigmoid_pre = jax.nn.sigmoid(pre_act)
    slope = sigmoid_pre * (1.0 + pre_act * (1.0 - sigmoid_pre))
    total_grad = fine_grad.reshape(BRICKS, C, EDGE, EDGE, EDGE).astype(jnp.float32) + up_grad
    pre_grad = (total_grad * slope).astype(jnp.bfloat16)
    padded_grad = pad_all(pre_grad.reshape(volume_shape), send_grid, recv_grid, z_grid).reshape(block_shape)
    flipped = conv_weight.reshape(3, 3, 3, C, C)[::-1, ::-1, ::-1].transpose(4, 3, 0, 1, 2)
    grad_in = lax.map(lambda region_block: conv_valid(region_block, flipped, forward_numbers), padded_grad)
    grad_in = grad_in.reshape(BRICKS, C, VOX).astype(jnp.bfloat16)
    weight_numbers = ('CNDHW', 'IODHW', 'NCDHW')
    pre_blocks = pre_grad.reshape(regions, owners * brick_slots, C, EDGE, EDGE, EDGE)
    weight_terms = lax.map(lambda region_items: conv_valid(region_items[0], region_items[1], weight_numbers), (padded_blocks, pre_blocks))
    factor = 1.0 / math.sqrt(BRICKS * VOX)
    grad_conv = lax.optimization_barrier(jnp.sum(weight_terms, axis=0)).transpose(2, 3, 4, 1, 0).reshape(27, C, C) * factor
    grad_down = lax.optimization_barrier(jnp.sum(down_terms, axis=0)).reshape(C2, 8, C).transpose(1, 0, 2) * factor
    return (fine_out.reshape(BRICKS, C, VOX), coarse_out, grad_in, grad_conv, grad_down)
```

```python
import math

import jax
import jax.numpy as jnp
import numpy as np
from jax import lax
from jax.experimental import pallas as pl
from jax.experimental.pallas import tpu as pltpu
from jax.sharding import PartitionSpec as P


C = 64
C2 = 128
VOX = 1728
B = 4
PROWS = 14 * 7 * 8
ROWS = 6 * 6 * 16
TAPS = 12
OFFSETS = (1, -1, 2, -2)
N_OWNER = 32
N_REGION = 8
CHUNK = 48
GROWS = N_OWNER * CHUNK
BF = jnp.bfloat16
F32 = jnp.float32
MESH = pl.DeviceIdType.MESH
VMEM_LIMIT = 56 * 1024 * 1024


def select_in(padded):
    count = 7 if padded else 6
    back = 1 if padded else 0
    out = np.zeros((8, 4, count * 8, 256), np.float32)
    for v in range(8):
        for e in range(2):
            for f in range(2):
                for jj in range(count):
                    for ll in range(count):
                        j, l = 2 * jj + e - back, 2 * ll + f - back
                        if 0 <= j < 12 and 0 <= l < 12:
                            col = 16 * v + j * 12 + l
                            if col < 256:
                                out[v, 2 * e + f, jj * 8 + ll, col] = 1
    return out.reshape(8, 4 * count * 8, 256).astype(BF)


def select_out():
    out = np.zeros((2, 2, 128, 288), np.float32)
    for e in range(2):
        for f in range(2):
            for jj in range(6):
                for s in range(2):
                    for ll in range(6):
                        out[e, f, jj * 16 + s * 8 + ll, s * 144 + (2 * jj + e) * 12 + 2 * ll + f] = 1
    return out.reshape(2, 256, 288).astype(BF)


def coarse_selects():
    down = np.zeros((768, 216), np.float32)
    up = np.zeros((288, 216), np.float32)
    spread = np.zeros((216, 2 * ROWS), np.float32)
    for ii in range(6):
        for jj in range(6):
            for ll in range(6):
                cell = ii * 36 + jj * 6 + ll
                down[ii * 128 + jj * 16 + ll, cell] = 1
                up[(ii * 6 + jj) * 8 + ll, cell] = 1
                for s in range(2):
                    spread[cell, s * ROWS + (ii * 6 + jj) * 16 + s * 8 + ll] = 1
    return down.astype(BF), up.astype(BF), spread.astype(BF)


def octant_swap():
    out = np.zeros((256, 256), np.float32)
    for q in range(8):
        for c in range(32):
            out[q * 32 + c, c * 8 + q] = 1
    return out.astype(BF)


def dot(a, b):
    return jnp.dot(a, b, preferred_element_type=F32)


def dot_t(a, b):
    return lax.dot_general(a, b, (((1,), (1,)), ((), ())), preferred_element_type=F32)


def low_lanes(rows):
    return lax.broadcasted_iota(jnp.int32, (rows, 128), 1) < 64


def to_rows(src_ref, sel_ref, count, put):
    nr = count * 8
    low = low_lanes(nr)
    for i in range(12):
        start = (144 * i) // 128 * 128
        width = min(256, VOX - start)
        window = src_ref[:, :, start : start + width].reshape(B * C, width)
        rows = dot_t(sel_ref[i % 8, :, :width], window)
        for e in range(2):
            for pair in range(2):
                lanes = slice(pair * 128, pair * 128 + 128)
                first = rows[2 * e * nr : (2 * e + 1) * nr, lanes]
                second = rows[(2 * e + 1) * nr : (2 * e + 2) * nr, lanes]
                put(2 * pair, i, e, jnp.where(low, first, pltpu.roll(second, 64, 1)))
                put(2 * pair + 1, i, e, jnp.where(low, pltpu.roll(first, 64, 1), second))


def from_rows(turned, sel_ref):
    total = None
    for e in range(2):
        blocks = [
            jnp.concatenate(
                [turned[(2 * e + f) * 64 : (2 * e + f + 1) * 64, ii * 128 : ii * 128 + 128] for f in range(2)], axis=1
            )
            for ii in range(6)
        ]
        part = dot(jnp.concatenate(blocks, axis=0), sel_ref[e])
        total = part if total is None else total + part
    return jnp.concatenate([total[ii * 64 : ii * 64 + 64] for ii in range(6)], axis=1)


def im2col(pad_ref, b, put):
    def step(ii, carry):
        for e in range(2):
            slabs = pad_ref[b, e, pl.ds(pl.multiple_of(ii * 112, 8), 224), :]
            shifted = pltpu.roll(slabs, 223, 0)
            for a in range(3):
                for dj in range(2):
                    for dl, source in ((0, slabs), (1, shifted)):
                        pieces = []
                        for jj in range(6):
                            for s in range(2):
                                row = ((a + s) * 7 + jj + dj) * 8
                                pieces.append(source[row : row + 8])
                        put(ii, ((a * 2 + dj) * 2 + dl) * 2 + e, jnp.concatenate(pieces, axis=0).astype(BF))
        return carry

    lax.fori_loop(0, 6, step, 0)


class Rounds:
    def __init__(self, pad, send_list, recv_list, z_list, bufs):
        self.pad, self.send_list, self.recv_list, self.z_list = pad, send_list, recv_list, z_list
        (self.sx, self.rx, self.sy, self.ry, self.sz, self.rz, self.ssem, self.rsem) = bufs
        self.region = lax.axis_index("region")
        self.owner = lax.axis_index("owner")

    def owner_copies(self, send, recv, base):
        out = []
        for m, t in enumerate(OFFSETS):
            out.append(
                pltpu.make_async_remote_copy(
                    src_ref=send.at[pl.ds(2 * m, 2)],
                    dst_ref=recv.at[pl.ds(2 * m, 2)],
                    send_sem=self.ssem.at[base + m],
                    recv_sem=self.rsem.at[base + m],
                    device_id=(self.region, lax.rem(self.owner + (t + N_OWNER), N_OWNER)),
                    device_id_type=MESH,
                )
            )
        return out

    def x_copies(self):
        return self.owner_copies(self.sx, self.rx, 0)

    def y_copies(self):
        return self.owner_copies(self.sy, self.ry, 4)

    def z_copies(self):
        out = []
        for m, t in enumerate((1, N_REGION - 1)):
            out.append(
                pltpu.make_async_remote_copy(
                    src_ref=self.sz.at[pl.ds(4 * m, 4)],
                    dst_ref=self.rz.at[pl.ds(4 * m, 4)],
                    send_sem=self.ssem.at[8 + m],
                    recv_sem=self.rsem.at[8 + m],
                    device_id=(lax.rem(self.region + t, N_REGION), self.owner),
                    device_id_type=MESH,
                )
            )
        return out

    def x_start(self):
        for n in range(8):
            pick = self.send_list[0, 0, n // 2, n % 2]
            slot, high = lax.rem(pick, 4), pick >= 4
            for e in range(2):
                low_face = self.pad[slot, e, 56:112, :]
                high_face = self.pad[slot, e, 672:728, :]
                self.sx[n, :, e * 128 : e * 128 + 128] = jnp.where(high, high_face, low_face).astype(BF)
        for copy in self.x_copies():
            copy.start()

    def x_end(self):
        for copy in self.x_copies():
            copy.wait_recv()
        for b in range(B):
            low_pad = self.rx[jnp.maximum(self.recv_list[b, 0, 0] - 8, 0)].astype(F32)
            high_pad = self.rx[jnp.maximum(self.recv_list[b, 0, 1] - 8, 0)].astype(F32)
            for e in range(2):
                self.pad[b, e, 0:56, :] = low_pad[:, e * 128 : e * 128 + 128]
                self.pad[b, e, 728:784, :] = high_pad[:, e * 128 : e * 128 + 128]

    def y_start(self):
        for n in range(8):
            pick = self.send_list[0, 1, n // 2, n % 2]
            slot, high = lax.rem(pick, 4), pick >= 4
            faces = []
            for i in range(14):
                low_face = self.pad[slot, 1, i * 56 : i * 56 + 8, :]
                high_face = self.pad[slot, 0, i * 56 + 48 : i * 56 + 56, :]
                faces.append(jnp.where(high, high_face, low_face))
            self.sy[n] = jnp.concatenate(faces, axis=0).astype(BF)
        for copy in self.y_copies():
            copy.start()

    def y_end(self):
        for copy in self.y_copies():
            copy.wait_recv()
        for b in range(B):
            low_pad = self.ry[jnp.maximum(self.recv_list[b, 1, 0] - 8, 0)].astype(F32)
            high_pad = self.ry[jnp.maximum(self.recv_list[b, 1, 1] - 8, 0)].astype(F32)
            for i in range(14):
                self.pad[b, 0, i * 56 : i * 56 + 8, :] = low_pad[i * 8 : i * 8 + 8]
                self.pad[b, 1, i * 56 + 48 : i * 56 + 56, :] = high_pad[i * 8 : i * 8 + 8]

    def z_start(self):
        low = low_lanes(98)
        for b in range(B):
            tiles = [self.pad[b, e, pl.ds(6, 98, stride=8), :] for e in range(2)]
            self.sz[b] = jnp.where(low, tiles[0], pltpu.roll(tiles[1], 64, 1)).astype(BF)
            tiles = [self.pad[b, e, pl.ds(0, 98, stride=8), :] for e in range(2)]
            self.sz[4 + b] = jnp.where(low, pltpu.roll(tiles[0], 64, 1), tiles[1]).astype(BF)
        for copy in self.z_copies():
            copy.start()

    def z_end(self):
        for copy in self.z_copies():
            copy.wait_recv()
        low = low_lanes(98)
        for b in range(B):
            for side in range(2):
                pick = self.z_list[b, side]
                zero = (pick == 8) | ((pick < 4) & (self.region == 0)) | ((pick >= 4) & (self.region == N_REGION - 1))
                face = self.rz[jnp.minimum(pick, 7)].astype(F32)
                face = jnp.where(zero, jnp.zeros_like(face), face)
                turned = pltpu.roll(face, 64, 1)
                row = 6 * side
                for e in range(2):
                    at = (b, e, pl.ds(row, 98, stride=8))
                    tile = self.pad[at]
                    if side == 0:
                        self.pad[at] = jnp.where(low, turned if e else face, tile)
                    else:
                        self.pad[at] = jnp.where(low, tile, face if e else turned)

    def drain(self):
        for copy in self.x_copies() + self.y_copies() + self.z_copies():
            copy.wait_send()


def round_scratch():
    return [
        pltpu.VMEM((8, 56, 256), BF),
        pltpu.VMEM((8, 56, 256), BF),
        pltpu.VMEM((8, 112, 128), BF),
        pltpu.VMEM((8, 112, 128), BF),
        pltpu.VMEM((8, 98, 128), BF),
        pltpu.VMEM((8, 98, 128), BF),
        pltpu.SemaphoreType.DMA((10,)),
        pltpu.SemaphoreType.DMA((10,)),
    ]


def meet(owners, regions):
    region, owner = lax.axis_index("region"), lax.axis_index("owner")
    barrier = pltpu.get_barrier_semaphore()
    for t in owners:
        pl.semaphore_signal(
            barrier, inc=1, device_id=(region, lax.rem(owner + (t + N_OWNER), N_OWNER)), device_id_type=MESH
        )
    for t in regions:
        pl.semaphore_signal(
            barrier, inc=1, device_id=(lax.rem(region + (t + N_REGION), N_REGION), owner), device_id_type=MESH
        )
    pl.semaphore_wait(barrier, len(owners) + len(regions))


def meet_all():
    region, owner = lax.axis_index("region"), lax.axis_index("owner")
    barrier = pltpu.get_barrier_semaphore()

    def one_owner(d, carry):
        pl.semaphore_signal(barrier, inc=1, device_id=(region, lax.rem(owner + d, N_OWNER)), device_id_type=MESH)
        return carry

    def one_region(d, carry):
        pl.semaphore_signal(barrier, inc=1, device_id=(lax.rem(region + d, N_REGION), owner), device_id_type=MESH)
        return carry

    lax.fori_loop(1, N_OWNER, one_owner, 0)
    lax.fori_loop(1, N_REGION, one_region, 0)
    pl.semaphore_wait(barrier, N_OWNER + N_REGION - 2)


def gather_kernel(
    feat, coarse, send_list, recv_list, z_list, p_send, p_recv, sel_in, swap, pad, child, octs, csend, crecv, cs, cr, *bufs
):
    region, owner = lax.axis_index("region"), lax.axis_index("owner")
    meet((1, -1, 2, -2, 3, -3, 4, -4), (1, -1))
    rounds = Rounds(pad, send_list, recv_list, z_list, bufs)

    def put(b, i, e, value):
        pad[b, e, (i + 1) * 56 : (i + 2) * 56, :] = value

    to_rows(feat, sel_in, 7, put)
    rounds.x_start()
    for g in range(4):
        rows = dot(swap[...], coarse[g * 256 : g * 256 + 256, :]).astype(BF)
        for q in range(8):
            octs[q, g * 32 : g * 32 + 32, :] = rows[q * 32 : q * 32 + 32]
    copies = []
    for m in range(4):
        index = jnp.int32(0)
        for q in range(8):
            index = jnp.where(p_recv[0, q] == m, q, index)
        csend[m] = octs[index]
        copies.append(
            pltpu.make_async_remote_copy(
                src_ref=csend.at[m],
                dst_ref=crecv.at[m],
                send_sem=cs.at[m],
                recv_sem=cr.at[m],
                device_id=(region, lax.rem(owner + (N_OWNER - m - 1), N_OWNER)),
                device_id_type=MESH,
            )
        )
    for copy in copies:
        copy.start()
    rounds.x_end()
    rounds.y_start()
    rounds.y_end()
    rounds.z_start()
    for copy in copies:
        copy.wait_recv()
    for k in range(B):
        index = jnp.int32(0)
        for m in range(4):
            index = jnp.where(p_send[0, m] == k, m, index)
        child[k] = crecv[index]
    rounds.z_end()
    rounds.drain()
    for copy in copies:
        copy.wait_send()


def compute_kernel(
    pad, fgrad, child, weight, down, sel_fg, sel_out, sel_down, sel_up, sel_spread, eye,
    fine, contrib, pre, grads,
    cols, wide, lhs, fg, fine8, turned, spread, fine_rows,
):
    zero = jnp.zeros((64, 64), BF)
    for e1 in range(2):
        for f1 in range(2):
            for a in range(3):
                for dj in range(2):
                    for dl in range(2):
                        for e in range(2):
                            te = 2 * dj + e - e1
                            blocks = []
                            for f in range(2):
                                tf = 2 * dl + f - f1
                                ok = 0 <= te < 3 and 0 <= tf < 3
                                blocks.append(weight[9 * a + 3 * te + tf] if ok else zero)
                            lane = ((a * 2 + dj) * 2 + dl) * 256 + e * 128
                            row = (2 * e1 + f1) * 64
                            wide[row : row + 64, lane : lane + 128] = jnp.concatenate(blocks, axis=1)
    lhs[0:256, :] = eye[...]
    for s in range(2):
        for e in range(2):
            pair = [down[4 * s + 2 * e + f] for f in range(2)]
            lhs[256 + s * 128 : 384 + s * 128, e * 128 : e * 128 + 128] = jnp.concatenate(pair, axis=1)

    def put_grad(b, i, e, value):
        for jj in range(6):
            row = ((i // 2) * 6 + jj) * 16 + (i % 2) * 8
            fg[b, row : row + 8, e * 128 : e * 128 + 128] = value[jj * 8 : jj * 8 + 8]

    to_rows(fgrad, sel_fg, 6, put_grad)
    for ii in range(6):
        fine8[ii * 128 + 96 : ii * 128 + 128, :] = jnp.zeros((32, 256), BF)
    live = lax.rem(lax.broadcasted_iota(jnp.int32, (ROWS, 256), 0), 8) < 6

    def brick(b, carry):
        base = pl.multiple_of(b * ROWS, 16)

        def put(ii, k, value):
            cols[pl.ds(pl.multiple_of(base + ii * 96, 16), 96), k * 128 : k * 128 + 128] = value

        im2col(pad, b, put)
        act = dot_t(cols[pl.ds(base, ROWS), :], wide[...])
        sig = 1.0 / (1.0 + jnp.exp(-act))
        rows = (act * sig).astype(BF)
        fine_rows[pl.ds(base, ROWS), :] = rows
        for ii in range(6):
            fine8[ii * 128 : ii * 128 + 96, :] = rows[ii * 96 : ii * 96 + 96]
        slope = sig * (1.0 + act * (1.0 - sig))
        kid = child[b]
        up_rows = dot_t(sel_up[...], kid).astype(BF)
        halves = [dot(up_rows, lhs[256 + s * 128 : 384 + s * 128, :]) for s in range(2)]
        pieces = []
        for t in range(36):
            for s in range(2):
                pieces.append(halves[s][t * 8 : t * 8 + 8])
        grad = (fg[b] + jnp.concatenate(pieces, axis=0)) * slope
        grad = jnp.where(live, grad, 0.0).astype(BF)
        pre[b] = grad
        turned[b] = dot_t(lhs[0:256, :], grad).astype(BF)
        for s in range(2):
            spread[b, s * 128 : s * 128 + 128, :] = dot(kid, sel_spread[:, s * ROWS : (s + 1) * ROWS]).astype(BF)
        both = dot_t(lhs[...], fine8[...])
        fine[b] = from_rows(both[0:256].astype(BF), sel_out).astype(BF)
        sums = both[256:384] + pltpu.roll(both[384:512], 760, 1)
        contrib[b] = dot(sums.astype(BF), sel_down[...]).astype(BF)
        return carry

    lax.fori_loop(0, B, brick, 0)

    low = low_lanes(64)
    main = [[None] * 3 for _ in range(3)]
    last = [[None] * 3 for _ in range(3)]

    def add(total, value):
        return value if total is None else total + value

    for a in range(3):
        for dj in range(2):
            tiles = []
            for dl in range(2):
                k = (a * 2 + dj) * 2 + dl
                total = None
                for b in range(B):
                    total = add(total, dot(turned[b], cols[b * ROWS : (b + 1) * ROWS, k * 256 : k * 256 + 256]))
                tiles.append(total)
            for e1 in range(2):
                for e in range(2):
                    te = 2 * dj + e - e1
                    if not 0 <= te < 3:
                        continue
                    lanes = slice(e * 128, e * 128 + 128)
                    t0, t1 = (tiles[dl][e1 * 128 : e1 * 128 + 64, lanes] for dl in range(2))
                    main[a][te] = add(main[a][te], t0)
                    last[a][te] = add(last[a][te], t1)
                    t0, t1 = (pltpu.roll(tiles[dl][e1 * 128 + 64 : e1 * 128 + 128, lanes], 64, 1) for dl in range(2))
                    main[a][te] = add(main[a][te], jnp.where(low, t0, t1))
                    last[a][te] = add(last[a][te], t1)
    main = main[0] + main[1] + main[2]
    last = last[0] + last[1] + last[2]
    for n in range(9):
        grads[n * 64 : n * 64 + 64, :] = main[n]
    for n in range(5):
        other = pltpu.roll(last[2 * n + 1], 64, 1) if n < 4 else jnp.zeros((64, 128), F32)
        grads[576 + n * 64 : 640 + n * 64, :] = jnp.where(low, last[2 * n], other)
    total = None
    for b in range(B):
        total = add(total, dot(spread[b], fine_rows[b * ROWS : (b + 1) * ROWS, :]))
    for e in range(2):
        grads[896 + e * 256 : 1152 + e * 256, :] = total[:, e * 128 : e * 128 + 128]
    grads[1408:1536, :] = jnp.zeros((128, 128), F32)


def reduce_kernel(
    pre, contrib, grads, send_list, recv_list, z_list, p_send, p_recv, swap,
    pad_out, coarse, conv_out, down_out,
    pad, csend, crecv, cs, cr, first, second, third, s1, r1, s2, r2, s3, r3, *bufs,
):
    region, owner = lax.axis_index("region"), lax.axis_index("owner")
    meet_all()
    rounds = Rounds(pad, send_list, recv_list, z_list, bufs)

    def leg1(d):
        to = lax.rem(owner + d, N_OWNER)
        return pltpu.make_async_remote_copy(
            src_ref=grads.at[to], dst_ref=first.at[d], send_sem=s1.at[d], recv_sem=r1.at[d],
            device_id=(region, to), device_id_type=MESH,
        )

    def leg2(d):
        return pltpu.make_async_remote_copy(
            src_ref=second.at[region], dst_ref=second.at[region], send_sem=s2.at[d], recv_sem=r2.at[d],
            device_id=(lax.rem(region + d, N_REGION), owner), device_id_type=MESH,
        )

    def leg3(d):
        return pltpu.make_async_remote_copy(
            src_ref=third.at[owner], dst_ref=third.at[owner], send_sem=s3.at[d], recv_sem=r3.at[d],
            device_id=(region, lax.rem(owner + d, N_OWNER)), device_id_type=MESH,
        )

    def each(count, leg, what):
        def body(d, carry):
            getattr(leg(d), what)()
            return carry

        lax.fori_loop(1, count, body, 0)

    low = low_lanes(48)
    edge = jnp.zeros((8, 128), F32)
    for b in range(B):
        for e in range(2):
            pad[b, e, 0:56, :] = jnp.zeros((56, 128), F32)
            pad[b, e, 728:784, :] = jnp.zeros((56, 128), F32)
    for b in range(B):

        def slab(ii, carry):
            rows = pre[b, pl.ds(pl.multiple_of(ii * 96, 16), 96), :].astype(F32)
            for s in range(2):
                to = pl.multiple_of((2 * ii + s + 1) * 56, 8)
                for e in range(2):
                    tile = jnp.concatenate(
                        [rows[jj * 16 + s * 8 : jj * 16 + s * 8 + 8, e * 128 : e * 128 + 128] for jj in range(6)], axis=0
                    )
                    tile = pltpu.roll(tile, 64, 1)
                    tile = jnp.where(low, pltpu.roll(tile, 1, 0), tile)
                    if e == 0:
                        pad[b, 1, pl.ds(to, 48), :] = tile
                        pad[b, 1, pl.ds(to + 48, 8), :] = edge
                    else:
                        pad[b, 0, pl.ds(to + 8, 48), :] = tile
                        pad[b, 0, pl.ds(to, 8), :] = edge
            return carry

        lax.fori_loop(0, 6, slab, 0)
    rounds.x_start()
    copies = []
    for m in range(4):
        csend[m] = contrib[p_send[0, m]]
        copies.append(
            pltpu.make_async_remote_copy(
                src_ref=csend.at[m], dst_ref=crecv.at[m], send_sem=cs.at[m], recv_sem=cr.at[m],
                device_id=(region, lax.rem(owner + (m + 1), N_OWNER)), device_id_type=MESH,
            )
        )
    for copy in copies:
        copy.start()
    each(N_OWNER, leg1, "start")
    rounds.x_end()
    rounds.y_start()
    rounds.y_end()
    rounds.z_start()
    for copy in copies:
        copy.wait_recv()
    crecv[4] = jnp.zeros((C2, 216), BF)
    parts = [crecv[p_recv[0, q]] for q in range(8)]
    for g in range(4):
        rows = jnp.concatenate([part[g * 32 : g * 32 + 32] for part in parts], axis=0)
        turned = lax.dot_general(swap[...], rows, (((0,), (0,)), ((), ())), preferred_element_type=F32)
        coarse[g * 256 : g * 256 + 256, :] = turned.astype(BF)
    rounds.z_end()
    pad_out[...] = pad[...]

    each(N_OWNER, leg1, "wait_recv")
    second[region] = lax.fori_loop(1, N_OWNER, lambda d, total: total + first[d], grads[owner])
    each(N_REGION, leg2, "start")
    each(N_REGION, leg2, "wait_recv")
    third[owner] = lax.fori_loop(1, N_REGION, lambda d, total: total + second[d], second[0])
    each(N_OWNER, leg3, "start")
    each(N_OWNER, leg3, "wait_recv")
    factor = 1.0 / math.sqrt(B * N_OWNER * N_REGION * VOX)
    total = third[...].reshape(GROWS, 128) * factor
    for n in range(9):
        tile = total[n * 64 : n * 64 + 64]
        conv_out[3 * n] = tile[:, 0:64]
        conv_out[3 * n + 1] = tile[:, 64:128]
        row = 576 + (n // 2) * 64
        conv_out[3 * n + 2] = total[row : row + 64, (n % 2) * 64 : (n % 2) * 64 + 64]
    for s in range(2):
        for e in range(2):
            row = 896 + e * 256 + s * 128
            for f in range(2):
                down_out[4 * s + 2 * e + f] = total[row : row + 128, f * 64 : f * 64 + 64]
    rounds.drain()
    for copy in copies:
        copy.wait_send()
    each(N_OWNER, leg1, "wait_send")
    each(N_REGION, leg2, "wait_send")
    each(N_OWNER, leg3, "wait_send")


def back_kernel(pad, weight, sel_out, eye, grad_in, cols, tall, rows8):
    zero = jnp.zeros((64, 64), BF)
    for e1 in range(2):
        for a in range(3):
            for dj in range(2):
                for dl in range(2):
                    for e in range(2):
                        te = 2 * dj + e - e1
                        for f in range(2):
                            blocks = []
                            for f1 in range(2):
                                tf = 2 * dl + f - f1
                                ok = 0 <= te < 3 and 0 <= tf < 3
                                blocks.append(weight[9 * (2 - a) + 3 * (2 - te) + 2 - tf] if ok else zero)
                            row = ((a * 2 + dj) * 2 + dl) * 256 + (2 * e + f) * 64
                            tall[row : row + 64, e1 * 128 : e1 * 128 + 128] = jnp.concatenate(blocks, axis=1)
    for ii in range(6):
        rows8[ii * 128 + 96 : ii * 128 + 128, :] = jnp.zeros((32, 256), BF)

    def brick(b, carry):
        def put(ii, k, value):
            cols[pl.ds(pl.multiple_of(ii * 96, 16), 96), k * 128 : k * 128 + 128] = value

        im2col(pad, b, put)
        rows = dot(cols[...], tall[...]).astype(BF)
        for ii in range(6):
            rows8[ii * 128 : ii * 128 + 96, :] = rows[ii * 96 : ii * 96 + 96]
        grad_in[b] = from_rows(dot_t(eye[...], rows8[...]).astype(BF), sel_out).astype(BF)
        return carry

    lax.fori_loop(0, B, brick, 0)


VM = pl.BlockSpec(memory_space=pltpu.VMEM)
SM = pl.BlockSpec(memory_space=pltpu.SMEM)


def struct(shape, kind):
    return jax.ShapeDtypeStruct(shape, kind)


def local(
    features, conv_weight, down_weight, fine_grad, coarse_grad, face_send, face_recv, z_recv, parent_send, parent_recv
):
    sel_down, sel_up, sel_spread = coarse_selects()
    swap = jnp.asarray(octant_swap())
    eye = jnp.asarray(np.eye(256, dtype=np.float32).astype(BF))
    sel_out = jnp.asarray(select_out())
    lists = (face_send, face_recv, z_recv, parent_send, parent_recv)
    pad, child = pl.pallas_call(
        gather_kernel,
        out_shape=(struct((B, 2, PROWS, 128), F32), struct((B, C2, 216), BF)),
        in_specs=[VM, VM] + [SM] * 5 + [VM, VM],
        out_specs=(VM, VM),
        scratch_shapes=[
            pltpu.VMEM((8, C2, 216), BF),
            pltpu.VMEM((4, C2, 216), BF),
            pltpu.VMEM((4, C2, 216), BF),
            pltpu.SemaphoreType.DMA((4,)),
            pltpu.SemaphoreType.DMA((4,)),
        ]
        + round_scratch(),
        compiler_params=pltpu.CompilerParams(collective_id=0, has_side_effects=True, vmem_limit_bytes=VMEM_LIMIT),
        name="gather",
    )(features, coarse_grad.reshape(1024, 216), *lists, jnp.asarray(select_in(True)), swap)
    fine, contrib, pre, grads = pl.pallas_call(
        compute_kernel,
        out_shape=(
            struct((B, C, VOX), BF),
            struct((B, C2, 216), BF),
            struct((B, ROWS, 256), BF),
            struct((GROWS, 128), F32),
        ),
        in_specs=[VM] * 11,
        out_specs=(VM,) * 4,
        scratch_shapes=[
            pltpu.VMEM((B * ROWS, TAPS * 256), BF),
            pltpu.VMEM((256, TAPS * 256), BF),
            pltpu.VMEM((512, 256), BF),
            pltpu.VMEM((B, ROWS, 256), F32),
            pltpu.VMEM((768, 256), BF),
            pltpu.VMEM((B, 256, ROWS), BF),
            pltpu.VMEM((B, 256, ROWS), BF),
            pltpu.VMEM((B * ROWS, 256), BF),
        ],
        compiler_params=pltpu.CompilerParams(vmem_limit_bytes=VMEM_LIMIT),
        name="compute",
    )(
        pad, fine_grad, child, conv_weight, down_weight,
        jnp.asarray(select_in(False)), sel_out, jnp.asarray(sel_down), jnp.asarray(sel_up), jnp.asarray(sel_spread), eye,
    )
    padded_grad, coarse_out, grad_conv, grad_down = pl.pallas_call(
        reduce_kernel,
        out_shape=(
            struct((B, 2, PROWS, 128), F32),
            struct((1024, 216), BF),
            struct((27, C, C), F32),
            struct((8, C2, C), F32),
        ),
        in_specs=[VM] * 3 + [SM] * 5 + [VM],
        out_specs=(VM,) * 4,
        scratch_shapes=[
            pltpu.VMEM((B, 2, PROWS, 128), F32),
            pltpu.VMEM((4, C2, 216), BF),
            pltpu.VMEM((5, C2, 216), BF),
            pltpu.SemaphoreType.DMA((4,)),
            pltpu.SemaphoreType.DMA((4,)),
            pltpu.VMEM((N_OWNER, CHUNK, 128), F32),
            pltpu.VMEM((N_REGION, CHUNK, 128), F32),
            pltpu.VMEM((N_OWNER, CHUNK, 128), F32),
            pltpu.SemaphoreType.DMA((N_OWNER,)),
            pltpu.SemaphoreType.DMA((N_OWNER,)),
            pltpu.SemaphoreType.DMA((N_REGION,)),
            pltpu.SemaphoreType.DMA((N_REGION,)),
            pltpu.SemaphoreType.DMA((N_OWNER,)),
            pltpu.SemaphoreType.DMA((N_OWNER,)),
        ]
        + round_scratch(),
        compiler_params=pltpu.CompilerParams(collective_id=1, has_side_effects=True, vmem_limit_bytes=VMEM_LIMIT),
        name="reduce",
    )(pre, contrib, grads.reshape(N_OWNER, CHUNK, 128), *lists, swap)
    grad_in = pl.pallas_call(
        back_kernel,
        out_shape=struct((B, C, VOX), BF),
        in_specs=[VM] * 4,
        out_specs=VM,
        scratch_shapes=[
            pltpu.VMEM((ROWS, TAPS * 256), BF),
            pltpu.VMEM((TAPS * 256, 256), BF),
            pltpu.VMEM((768, 256), BF),
        ],
        compiler_params=pltpu.CompilerParams(vmem_limit_bytes=VMEM_LIMIT),
        name="back",
    )(padded_grad, conv_weight, sel_out, eye)
    return fine, coarse_out.reshape(1, C2, 8, 216), grad_in, grad_conv, grad_down


def solution(mesh):
    both = ("region", "owner")
    return jax.shard_map(
        local,
        mesh=mesh,
        in_specs=(
            P(both, None, None),
            P(),
            P(),
            P(both, None, None),
            P(both, None, None, None),
            P(both, None, None, None),
            P(both, None, None),
            P(both, None),
            P(both, None),
            P(both, None),
        ),
        out_specs=(P(both, None, None), P(both, None, None, None), P(both, None, None), P(), P()),
        check_vma=False,
    )
```

```python
import math

import jax
import jax.numpy as jnp
import numpy as np
from jax import lax
from jax.experimental import pallas as pl
from jax.experimental.pallas import tpu as pltpu
from jax.sharding import PartitionSpec as P


C = 64
C2 = 128
VOX = 1728
B = 4
PROWS = 14 * 7 * 8
ROWS = 6 * 6 * 16
TAPS = 12
OFFSETS = (1, -1, 2, -2)
N_OWNER = 32
N_REGION = 8
CHUNK = 48
GROWS = N_OWNER * CHUNK
BF = jnp.bfloat16
F32 = jnp.float32
MESH = pl.DeviceIdType.MESH
VMEM_LIMIT = 56 * 1024 * 1024


def select_in(padded):
    count = 7 if padded else 6
    back = 1 if padded else 0
    out = np.zeros((8, 4, count * 8, 256), np.float32)
    for v in range(8):
        for e in range(2):
            for f in range(2):
                for jj in range(count):
                    for ll in range(count):
                        j, l = 2 * jj + e - back, 2 * ll + f - back
                        if 0 <= j < 12 and 0 <= l < 12:
                            col = 16 * v + j * 12 + l
                            if col < 256:
                                out[v, 2 * e + f, jj * 8 + ll, col] = 1
    return out.reshape(8, 4 * count * 8, 256).astype(BF)


def select_out():
    out = np.zeros((2, 2, 128, 288), np.float32)
    for e in range(2):
        for f in range(2):
            for jj in range(6):
                for s in range(2):
                    for ll in range(6):
                        out[e, f, jj * 16 + s * 8 + ll, s * 144 + (2 * jj + e) * 12 + 2 * ll + f] = 1
    return out.reshape(2, 256, 288).astype(BF)


def coarse_selects():
    up = np.zeros((288, 216), np.float32)
    for ii in range(6):
        for jj in range(6):
            for ll in range(6):
                up[(ii * 6 + jj) * 8 + ll, ii * 36 + jj * 6 + ll] = 1
    return up.astype(BF), up.T.copy().astype(BF)


def dot(a, b):
    return jnp.dot(a, b, preferred_element_type=F32)


def dot_t(a, b):
    return lax.dot_general(a, b, (((1,), (1,)), ((), ())), preferred_element_type=F32)


def low_lanes(rows):
    return lax.broadcasted_iota(jnp.int32, (rows, 128), 1) < 64


def to_rows(src_ref, sel_ref, count, put):
    nr = count * 8
    low = low_lanes(nr)
    for i in range(12):
        start = (144 * i) // 128 * 128
        width = min(256, VOX - start)
        window = src_ref[:, :, start : start + width].reshape(B * C, width)
        rows = dot_t(sel_ref[i % 8, :, :width], window)
        for e in range(2):
            for pair in range(2):
                lanes = slice(pair * 128, pair * 128 + 128)
                first = rows[2 * e * nr : (2 * e + 1) * nr, lanes]
                second = rows[(2 * e + 1) * nr : (2 * e + 2) * nr, lanes]
                put(2 * pair, i, e, jnp.where(low, first, pltpu.roll(second, 64, 1)))
                put(2 * pair + 1, i, e, jnp.where(low, pltpu.roll(first, 64, 1), second))


def from_rows(turned, sel_ref):
    total = None
    for e in range(2):
        blocks = [
            jnp.concatenate(
                [turned[(2 * e + f) * 64 : (2 * e + f + 1) * 64, ii * 128 : ii * 128 + 128] for f in range(2)], axis=1
            )
            for ii in range(6)
        ]
        part = dot(jnp.concatenate(blocks, axis=0), sel_ref[e])
        total = part if total is None else total + part
    return jnp.concatenate([total[ii * 64 : ii * 64 + 64] for ii in range(6)], axis=1)


def im2col(pad_ref, b, put):
    def step(ii, carry):
        for e in range(2):
            slabs = pad_ref[b, e, pl.ds(pl.multiple_of(ii * 112, 8), 224), :]
            shifted = pltpu.roll(slabs, 223, 0)
            for a in range(3):
                for dj in range(2):
                    for dl, source in ((0, slabs), (1, shifted)):
                        pieces = []
                        for jj in range(6):
                            for s in range(2):
                                row = ((a + s) * 7 + jj + dj) * 8
                                pieces.append(source[row : row + 8])
                        put(ii, ((a * 2 + dj) * 2 + dl) * 2 + e, jnp.concatenate(pieces, axis=0).astype(BF))
        return carry

    lax.fori_loop(0, 6, step, 0)


class Rounds:
    def __init__(self, pad, send_list, recv_list, z_list, bufs):
        self.pad, self.send_list, self.recv_list, self.z_list = pad, send_list, recv_list, z_list
        (self.sx, self.rx, self.sy, self.ry, self.sz, self.rz, self.ssem, self.rsem) = bufs
        self.region = lax.axis_index("region")
        self.owner = lax.axis_index("owner")

    def owner_copies(self, send, recv, base):
        out = []
        for m, t in enumerate(OFFSETS):
            out.append(
                pltpu.make_async_remote_copy(
                    src_ref=send.at[pl.ds(2 * m, 2)],
                    dst_ref=recv.at[pl.ds(2 * m, 2)],
                    send_sem=self.ssem.at[base + m],
                    recv_sem=self.rsem.at[base + m],
                    device_id=(self.region, lax.rem(self.owner + (t + N_OWNER), N_OWNER)),
                    device_id_type=MESH,
                )
            )
        return out

    def x_copies(self):
        return self.owner_copies(self.sx, self.rx, 0)

    def y_copies(self):
        return self.owner_copies(self.sy, self.ry, 4)

    def z_copies(self):
        out = []
        for m, t in enumerate((1, N_REGION - 1)):
            out.append(
                pltpu.make_async_remote_copy(
                    src_ref=self.sz.at[pl.ds(4 * m, 4)],
                    dst_ref=self.rz.at[pl.ds(4 * m, 4)],
                    send_sem=self.ssem.at[8 + m],
                    recv_sem=self.rsem.at[8 + m],
                    device_id=(lax.rem(self.region + t, N_REGION), self.owner),
                    device_id_type=MESH,
                )
            )
        return out

    def x_start(self):
        for n in range(8):
            pick = self.send_list[0, 0, n % 2, n // 2]
            slot, high = lax.rem(pick, 4), pick >= 4
            for e in range(2):
                low_face = self.pad[slot, e, 56:112, :]
                high_face = self.pad[slot, e, 672:728, :]
                self.sx[n, :, e * 128 : e * 128 + 128] = jnp.where(high, high_face, low_face).astype(BF)
        for copy in self.x_copies():
            copy.start()

    def x_end(self):
        for copy in self.x_copies():
            copy.wait_recv()
        for b in range(B):
            low_pad = self.rx[jnp.maximum(self.recv_list[0, 0, b] - 8, 0)].astype(F32)
            high_pad = self.rx[jnp.maximum(self.recv_list[0, 1, b] - 8, 0)].astype(F32)
            for e in range(2):
                self.pad[b, e, 0:56, :] = low_pad[:, e * 128 : e * 128 + 128]
                self.pad[b, e, 728:784, :] = high_pad[:, e * 128 : e * 128 + 128]

    def y_start(self):
        for n in range(8):
            pick = self.send_list[0, 1, n % 2, n // 2]
            slot, high = lax.rem(pick, 4), pick >= 4
            faces = []
            for i in range(14):
                low_face = self.pad[slot, 1, i * 56 : i * 56 + 8, :]
                high_face = self.pad[slot, 0, i * 56 + 48 : i * 56 + 56, :]
                faces.append(jnp.where(high, high_face, low_face))
            self.sy[n] = jnp.concatenate(faces, axis=0).astype(BF)
        for copy in self.y_copies():
            copy.start()

    def y_end(self):
        for copy in self.y_copies():
            copy.wait_recv()
        for b in range(B):
            low_pad = self.ry[jnp.maximum(self.recv_list[1, 0, b] - 8, 0)].astype(F32)
            high_pad = self.ry[jnp.maximum(self.recv_list[1, 1, b] - 8, 0)].astype(F32)
            for i in range(14):
                self.pad[b, 0, i * 56 : i * 56 + 8, :] = low_pad[i * 8 : i * 8 + 8]
                self.pad[b, 1, i * 56 + 48 : i * 56 + 56, :] = high_pad[i * 8 : i * 8 + 8]

    def z_start(self):
        low = low_lanes(98)
        for b in range(B):
            tiles = [self.pad[b, e, pl.ds(6, 98, stride=8), :] for e in range(2)]
            self.sz[b] = jnp.where(low, tiles[0], pltpu.roll(tiles[1], 64, 1)).astype(BF)
            tiles = [self.pad[b, e, pl.ds(0, 98, stride=8), :] for e in range(2)]
            self.sz[4 + b] = jnp.where(low, pltpu.roll(tiles[0], 64, 1), tiles[1]).astype(BF)
        for copy in self.z_copies():
            copy.start()

    def z_end(self):
        for copy in self.z_copies():
            copy.wait_recv()
        low = low_lanes(98)
        for b in range(B):
            for side in range(2):
                pick = self.z_list[side, b]
                zero = (pick == 8) | ((pick < 4) & (self.region == 0)) | ((pick >= 4) & (self.region == N_REGION - 1))
                face = self.rz[jnp.minimum(pick, 7)].astype(F32)
                face = jnp.where(zero, jnp.zeros_like(face), face)
                turned = pltpu.roll(face, 64, 1)
                row = 6 * side
                for e in range(2):
                    at = (b, e, pl.ds(row, 98, stride=8))
                    tile = self.pad[at]
                    if side == 0:
                        self.pad[at] = jnp.where(low, turned if e else face, tile)
                    else:
                        self.pad[at] = jnp.where(low, tile, face if e else turned)

    def drain(self):
        for copy in self.x_copies() + self.y_copies() + self.z_copies():
            copy.wait_send()


def round_scratch():
    return [
        pltpu.VMEM((8, 56, 256), BF),
        pltpu.VMEM((8, 56, 256), BF),
        pltpu.VMEM((8, 112, 128), BF),
        pltpu.VMEM((8, 112, 128), BF),
        pltpu.VMEM((8, 98, 128), BF),
        pltpu.VMEM((8, 98, 128), BF),
        pltpu.SemaphoreType.DMA((10,)),
        pltpu.SemaphoreType.DMA((10,)),
    ]


class Barrier:
    def __init__(self):
        self.region, self.owner = lax.axis_index("region"), lax.axis_index("owner")
        self.barrier = pltpu.get_barrier_semaphore()

    def signal(self):
        def one_owner(d, carry):
            to = (self.region, lax.rem(self.owner + d, N_OWNER))
            pl.semaphore_signal(self.barrier, inc=1, device_id=to, device_id_type=MESH)
            return carry

        def one_region(d, carry):
            to = (lax.rem(self.region + d, N_REGION), self.owner)
            pl.semaphore_signal(self.barrier, inc=1, device_id=to, device_id_type=MESH)
            return carry

        lax.fori_loop(1, N_OWNER, one_owner, 0)
        lax.fori_loop(1, N_REGION, one_region, 0)

    def wait(self):
        pl.semaphore_wait(self.barrier, N_OWNER + N_REGION - 2)


def forward_weights(weight, wide):
    zero = jnp.zeros((64, 64), BF)
    for e1 in range(2):
        for f1 in range(2):
            for k in range(TAPS):
                a, dj, dl = k // 4, k // 2 % 2, k % 2
                for e in range(2):
                    te = 2 * dj + e - e1
                    blocks = []
                    for f in range(2):
                        tf = 2 * dl + f - f1
                        ok = 0 <= te < 3 and 0 <= tf < 3
                        blocks.append(weight[9 * a + 3 * te + tf] if ok else zero)
                    row, lane = (2 * e1 + f1) * 64, k * 256 + e * 128
                    wide[row : row + 64, lane : lane + 128] = jnp.concatenate(blocks, axis=1)


def backward_weights(weight, tall):
    zero = jnp.zeros((64, 64), BF)
    for e1 in range(2):
        for k in range(TAPS):
            a, dj, dl = k // 4, k // 2 % 2, k % 2
            for e in range(2):
                te = 2 * dj + e - e1
                for f in range(2):
                    blocks = []
                    for f1 in range(2):
                        tf = 2 * dl + f - f1
                        ok = 0 <= te < 3 and 0 <= tf < 3
                        blocks.append(weight[9 * (2 - a) + 3 * (2 - te) + 2 - tf] if ok else zero)
                    row = k * 256 + (2 * e + f) * 64
                    tall[row : row + 64, e1 * 128 : e1 * 128 + 128] = jnp.concatenate(blocks, axis=1)


def pad_rows(pad, b, rows):
    low = low_lanes(48)
    edge = jnp.zeros((8, 128), F32)
    for e in range(2):
        pad[b, e, 0:56, :] = jnp.zeros((56, 128), F32)
        pad[b, e, 728:784, :] = jnp.zeros((56, 128), F32)
    for ii in range(6):
        for s in range(2):
            to = (2 * ii + s + 1) * 56
            for e in range(2):
                tile = jnp.concatenate(
                    [
                        rows[ii * 96 + jj * 16 + s * 8 : ii * 96 + jj * 16 + s * 8 + 8, e * 128 : e * 128 + 128]
                        for jj in range(6)
                    ],
                    axis=0,
                )
                tile = pltpu.roll(tile, 64, 1)
                tile = jnp.where(low, pltpu.roll(tile, 1, 0), tile)
                if e == 0:
                    pad[b, 1, to : to + 48, :] = tile
                    pad[b, 1, to + 48 : to + 56, :] = edge
                else:
                    pad[b, 0, to + 8 : to + 56, :] = tile
                    pad[b, 0, to : to + 8, :] = edge


def fold_conv(turned, cols, grads):
    low = low_lanes(64)
    main = [[None] * 3 for _ in range(3)]
    last = [[None] * 3 for _ in range(3)]

    def add(total, value):
        return value if total is None else total + value

    for a in range(3):
        for dj in range(2):
            tiles = []
            for dl in range(2):
                k = (a * 2 + dj) * 2 + dl
                total = None
                for b in range(B):
                    total = add(total, dot(turned[b], cols[b * ROWS : (b + 1) * ROWS, k * 256 : k * 256 + 256]))
                tiles.append(total)
            for e1 in range(2):
                for e in range(2):
                    te = 2 * dj + e - e1
                    if not 0 <= te < 3:
                        continue
                    lanes = slice(e * 128, e * 128 + 128)
                    t0, t1 = (tiles[dl][e1 * 128 : e1 * 128 + 64, lanes] for dl in range(2))
                    main[a][te] = add(main[a][te], t0)
                    last[a][te] = add(last[a][te], t1)
                    t0, t1 = (pltpu.roll(tiles[dl][e1 * 128 + 64 : e1 * 128 + 128, lanes], 64, 1) for dl in range(2))
                    main[a][te] = add(main[a][te], jnp.where(low, t0, t1))
                    last[a][te] = add(last[a][te], t1)
    main = main[0] + main[1] + main[2]
    last = last[0] + last[1] + last[2]

    def put(row, value):
        for start, size, part, at in split_rows(row, 64):
            grads[part, at : at + size, :] = value[start : start + size]

    for n in range(9):
        put(n * 64, main[n])
    for n in range(5):
        other = pltpu.roll(last[2 * n + 1], 64, 1) if n < 4 else jnp.zeros((64, 128), F32)
        put(576 + n * 64, jnp.where(low, last[2 * n], other))


def split_rows(row, count):
    out, start = [], 0
    while start < count:
        part, at = divmod(row + start, CHUNK)
        size = min(count - start, CHUNK - at)
        out.append((start, size, part, at))
        start += size
    return out


def step_kernel(
    feat, weight, down, fgrad, coarse_in, send_list, recv_list, z_list, p_send, p_recv,
    sel_in, sel_fg, sel_out, sel_up, sel_down, eye,
    fine, coarse, grad_in, conv_out, down_out,
    pad, cols, wide, tall, mats, fg, rows8, turned, grad_turned, kids, child, grads,
    csend, crecv, dsend, drecv, first, second, mine, third, cs, cr, ds, dr, s1, r1, s2, r2, s3, r3, *bufs,
):
    region, owner = lax.axis_index("region"), lax.axis_index("owner")
    barrier = Barrier()
    barrier.signal()
    half = len(bufs) // 2
    ahead = Rounds(pad, send_list, recv_list, z_list, bufs[:half])
    back = Rounds(pad, send_list, recv_list, z_list, bufs[half:])

    def to_owner(src, dst, send, recv, shift):
        return pltpu.make_async_remote_copy(
            src_ref=src, dst_ref=dst, send_sem=send, recv_sem=recv,
            device_id=(region, lax.rem(owner + shift, N_OWNER)), device_id_type=MESH,
        )

    def leg1(d):
        return to_owner(grads.at[lax.rem(owner + d, N_OWNER)], first.at[d], s1.at[d], r1.at[d], d)

    def leg2(d):
        return pltpu.make_async_remote_copy(
            src_ref=second.at[region], dst_ref=second.at[region], send_sem=s2.at[d], recv_sem=r2.at[d],
            device_id=(lax.rem(region + d, N_REGION), owner), device_id_type=MESH,
        )

    def leg3(d):
        return to_owner(mine, third.at[owner], s3.at[d], r3.at[d], d)

    def each(count, leg, what):
        def body(d, carry):
            getattr(leg(d), what)()
            return carry

        lax.fori_loop(1, count, body, 0)

    def put(b, i, e, value):
        pad[b, e, (i + 1) * 56 : (i + 2) * 56, :] = value

    to_rows(feat, sel_in, 7, put)
    barrier.wait()
    ahead.x_start()
    kid_copies = [to_owner(csend.at[m], crecv.at[m], cs.at[m], cr.at[m], N_OWNER - m - 1) for m in range(4)]
    for m in range(4):
        index = jnp.int32(0)
        for q in range(8):
            index = jnp.where(p_recv[0, q] == m, q, index)
        csend[m] = coarse_in[index]
        kid_copies[m].start()
    forward_weights(weight, wide)
    ahead.x_end()
    ahead.y_start()

    def put_grad(b, i, e, value):
        for jj in range(6):
            row = ((i // 2) * 6 + jj) * 16 + (i % 2) * 8
            fg[b, row : row + 8, e * 128 : e * 128 + 128] = value[jj * 8 : jj * 8 + 8]

    to_rows(fgrad, sel_fg, 6, put_grad)
    ahead.y_end()
    ahead.z_start()
    for s in range(2):
        mats[s] = jnp.concatenate([down[4 * s + n] for n in range(4)], axis=0)
    for b in range(B):
        for ii in range(6):
            rows8[b, ii * 128 + 96 : ii * 128 + 128, :] = jnp.zeros((32, 256), BF)
    for copy in kid_copies:
        copy.wait_recv()
    for k in range(B):
        index = jnp.int32(0)
        for m in range(4):
            index = jnp.where(p_send[0, m] == k, m, index)
        child[k] = crecv[index]
    backward_weights(weight, tall)
    ahead.z_end()

    live = lax.rem(lax.broadcasted_iota(jnp.int32, (ROWS, 256), 0), 8) < 6
    blank = jnp.zeros((8, 128), F32)

    def brick(b, carry):
        base = pl.multiple_of(b * ROWS, 16)

        def put(ii, k, value):
            cols[pl.ds(pl.multiple_of(base + ii * 96, 16), 96), k * 128 : k * 128 + 128] = value

        im2col(pad, b, put)
        act = dot_t(cols[pl.ds(base, ROWS), :], wide[...])
        sig = 1.0 / (1.0 + jnp.exp(-act))
        rows = (act * sig).astype(BF)
        for ii in range(6):
            rows8[b, ii * 128 : ii * 128 + 96, :] = rows[ii * 96 : ii * 96 + 96]
        slope = sig * (1.0 + act * (1.0 - sig))
        up = dot(sel_up[...], child[b])
        halves = [dot_t(up.astype(BF), mats[s]) for s in range(2)]
        pieces, kid = [], []
        for t in range(36):
            cut = up[t * 8 : t * 8 + 8]
            kid += [jnp.concatenate([cut, blank], axis=1), jnp.concatenate([blank, cut], axis=1)]
            for s in range(2):
                pieces.append(halves[s][t * 8 : t * 8 + 8])
        kids[pl.ds(base, ROWS), :] = jnp.concatenate(kid, axis=0).astype(BF)
        grad = (fg[b] + jnp.concatenate(pieces, axis=0)) * slope
        grad = jnp.where(live, grad, 0.0).astype(BF)
        grad_turned[b] = dot_t(eye[...], grad).astype(BF)
        pad_rows(pad, b, grad.astype(F32))
        return carry

    lax.fori_loop(0, B, brick, 0)
    back.x_start()

    def contribution(b, carry):
        pieces = [
            dot(jnp.concatenate([rows8[b, ii * 128 : ii * 128 + 96, :] for ii in range(6)], axis=0), mats[s])
            for s in range(2)
        ]
        sums = [pieces[0][t * 16 : t * 16 + 8] + pieces[1][t * 16 + 8 : t * 16 + 16] for t in range(36)]
        coarse_tmp = dot(sel_down[...], jnp.concatenate(sums, axis=0).astype(BF)).astype(BF)
        child[b] = coarse_tmp
        turned[b] = dot_t(eye[...], rows8[b]).astype(BF)
        return carry

    lax.fori_loop(0, B, contribution, 0)
    up_copies = [to_owner(dsend.at[m], drecv.at[m], ds.at[m], dr.at[m], m + 1) for m in range(4)]
    for m in range(4):
        dsend[m] = child[p_send[0, m]]
        up_copies[m].start()

    fold_conv(grad_turned, cols, grads)
    total = None
    for b in range(B):
        short = jnp.concatenate([turned[b, :, ii * 128 : ii * 128 + 96] for ii in range(6)], axis=1)
        part = dot(short, kids[b * ROWS : (b + 1) * ROWS, :])
        total = part if total is None else total + part
    for s in range(2):
        for start, size, part, at in split_rows(896 + s * 256, 256):
            grads[part, at : at + size, :] = total[start : start + size, s * 128 : s * 128 + 128]
    for start, size, part, at in split_rows(1408, 128):
        grads[part, at : at + size, :] = jnp.zeros((size, 128), F32)
    each(N_OWNER, leg1, "start")
    back.x_end()
    back.y_start()
    for b in range(2):
        fine[b] = from_rows(turned[b], sel_out).astype(BF)
    back.y_end()
    back.z_start()
    for b in range(2, B):
        fine[b] = from_rows(turned[b], sel_out).astype(BF)
    for copy in up_copies:
        copy.wait_recv()
    drecv[4] = jnp.zeros((216, C2), BF)
    for q in range(8):
        coarse[q] = drecv[p_recv[0, q]]
    back.z_end()

    def back_brick(b, carry):
        def put(ii, k, value):
            cols[pl.ds(pl.multiple_of(ii * 96, 16), 96), k * 128 : k * 128 + 128] = value

        im2col(pad, b, put)
        rows = dot(cols[pl.ds(0, ROWS), :], tall[...]).astype(BF)
        for ii in range(6):
            rows8[b, ii * 128 : ii * 128 + 96, :] = rows[ii * 96 : ii * 96 + 96]
        grad_in[b] = from_rows(dot_t(eye[...], rows8[b]).astype(BF), sel_out).astype(BF)
        return carry

    lax.fori_loop(0, 1, back_brick, 0)
    each(N_OWNER, leg1, "wait_recv")
    second[region] = lax.fori_loop(1, N_OWNER, lambda d, total: total + first[d], grads[owner])
    each(N_REGION, leg2, "start")
    lax.fori_loop(1, 3, back_brick, 0)
    each(N_REGION, leg2, "wait_recv")
    part = lax.fori_loop(1, N_REGION, lambda d, total: total + second[d], second[0])
    factor = 1.0 / math.sqrt(B * N_OWNER * N_REGION * VOX)
    part = (part * factor).astype(BF)
    mine[...] = part
    each(N_OWNER, leg3, "start")
    third[owner] = part
    lax.fori_loop(3, B, back_brick, 0)
    each(N_OWNER, leg3, "wait_recv")
    total = third[...].astype(F32).reshape(GROWS, 128)
    for n in range(9):
        tile = total[n * 64 : n * 64 + 64]
        conv_out[3 * n] = tile[:, 0:64]
        conv_out[3 * n + 1] = tile[:, 64:128]
        row = 576 + (n // 2) * 64
        conv_out[3 * n + 2] = total[row : row + 64, (n % 2) * 64 : (n % 2) * 64 + 64]
    for t in range(8):
        down_out[t] = total[896 + t * 64 : 960 + t * 64]
    ahead.drain()
    back.drain()
    for copy in kid_copies + up_copies:
        copy.wait_send()
    each(N_OWNER, leg1, "wait_send")
    each(N_REGION, leg2, "wait_send")
    each(N_OWNER, leg3, "wait_send")


VM = pl.BlockSpec(memory_space=pltpu.VMEM)
SM = pl.BlockSpec(memory_space=pltpu.SMEM)


def struct(shape, kind):
    return jax.ShapeDtypeStruct(shape, kind)


def local(
    features, conv_weight, down_weight, fine_grad, coarse_grad, face_send, face_recv, z_recv, parent_send, parent_recv
):
    sel_up, sel_down = coarse_selects()
    consts = (select_in(True), select_in(False), select_out(), sel_up, sel_down, np.eye(256, dtype=np.float32).astype(BF))
    dma = pltpu.SemaphoreType.DMA
    fine, coarse_out, grad_in, grad_conv, grad_down = pl.pallas_call(
        step_kernel,
        out_shape=(
            struct((B, C, VOX), BF),
            struct((8, 216, C2), BF),
            struct((B, C, VOX), BF),
            struct((27, C, C), F32),
            struct((8, C, C2), F32),
        ),
        in_specs=[VM] * 5 + [SM] * 5 + [VM] * 6,
        out_specs=(VM,) * 5,
        scratch_shapes=[
            pltpu.VMEM((B, 2, PROWS, 128), F32),
            pltpu.VMEM((B * ROWS, TAPS * 256), BF),
            pltpu.VMEM((256, TAPS * 256), BF),
            pltpu.VMEM((TAPS * 256, 256), BF),
            pltpu.VMEM((2, 256, C2), BF),
            pltpu.VMEM((B, ROWS, 256), F32),
            pltpu.VMEM((B, 768, 256), BF),
            pltpu.VMEM((B, 256, 768), BF),
            pltpu.VMEM((B, 256, ROWS), BF),
            pltpu.VMEM((B * ROWS, 256), BF),
            pltpu.VMEM((B, 216, C2), BF),
            pltpu.VMEM((N_OWNER, CHUNK, 128), F32),
            pltpu.VMEM((4, 216, C2), BF),
            pltpu.VMEM((4, 216, C2), BF),
            pltpu.VMEM((4, 216, C2), BF),
            pltpu.VMEM((5, 216, C2), BF),
            pltpu.VMEM((N_OWNER, CHUNK, 128), F32),
            pltpu.VMEM((N_REGION, CHUNK, 128), F32),
            pltpu.VMEM((CHUNK, 128), BF),
            pltpu.VMEM((N_OWNER, CHUNK, 128), BF),
        ]
        + [dma((4,))] * 4
        + [dma((N_OWNER,))] * 2
        + [dma((N_REGION,))] * 2
        + [dma((N_OWNER,))] * 2
        + round_scratch()
        + round_scratch(),
        compiler_params=pltpu.CompilerParams(collective_id=0, has_side_effects=True, vmem_limit_bytes=VMEM_LIMIT),
        name="step",
    )(
        features, conv_weight, down_weight.transpose(0, 2, 1), fine_grad, coarse_grad[0].transpose(1, 2, 0),
        face_send.transpose(0, 1, 3, 2), face_recv.transpose(1, 2, 0), z_recv.transpose(1, 0), parent_send, parent_recv,
        *(jnp.asarray(c) for c in consts),
    )
    return fine, coarse_out.transpose(2, 0, 1)[None], grad_in, grad_conv, grad_down.transpose(0, 2, 1)


def solution(mesh):
    both = ("region", "owner")
    return jax.shard_map(
        local,
        mesh=mesh,
        in_specs=(
            P(both, None, None),
            P(),
            P(),
            P(both, None, None),
            P(both, None, None, None),
            P(both, None, None, None),
            P(both, None, None),
            P(both, None),
            P(both, None),
            P(both, None),
        ),
        out_specs=(P(both, None, None), P(both, None, None, None), P(both, None, None), P(), P()),
        check_vma=False,
    )
```

```python
import math

import jax
import jax.numpy as jnp
import numpy as np
from jax import lax
from jax.experimental import pallas as pl
from jax.experimental.pallas import tpu as pltpu
from jax.sharding import PartitionSpec as P


C = 64
C2 = 128
VOX = 1728
B = 4
PROWS = 14 * 7 * 8
ROWS = 6 * 6 * 16
TAPS = 12
OFFSETS = (1, -1, 2, -2)
N_OWNER = 32
N_REGION = 8
CHUNK = 48
GROWS = N_OWNER * CHUNK
BF = jnp.bfloat16
F32 = jnp.float32
MESH = pl.DeviceIdType.MESH
VMEM_LIMIT = 56 * 1024 * 1024


def select_in(padded):
    count = 7 if padded else 6
    back = 1 if padded else 0
    out = np.zeros((8, 4, count * 8, 256), np.float32)
    for v in range(8):
        for e in range(2):
            for f in range(2):
                for jj in range(count):
                    for ll in range(count):
                        j, l = 2 * jj + e - back, 2 * ll + f - back
                        if 0 <= j < 12 and 0 <= l < 12:
                            col = 16 * v + j * 12 + l
                            if col < 256:
                                out[v, 2 * e + f, jj * 8 + ll, col] = 1
    return out.reshape(8, 4 * count * 8, 256).astype(BF)


def select_out():
    out = np.zeros((2, 2, 128, 288), np.float32)
    for e in range(2):
        for f in range(2):
            for jj in range(6):
                for s in range(2):
                    for ll in range(6):
                        out[e, f, jj * 16 + s * 8 + ll, s * 144 + (2 * jj + e) * 12 + 2 * ll + f] = 1
    return out.reshape(2, 256, 288).astype(BF)


def coarse_selects():
    up = np.zeros((288, 216), np.float32)
    for ii in range(6):
        for jj in range(6):
            for ll in range(6):
                up[(ii * 6 + jj) * 8 + ll, ii * 36 + jj * 6 + ll] = 1
    return up.astype(BF), up.T.copy().astype(BF)


def dot(a, b):
    return jnp.dot(a, b, preferred_element_type=F32)


def dot_t(a, b):
    return lax.dot_general(a, b, (((1,), (1,)), ((), ())), preferred_element_type=F32)


def low_lanes(rows):
    return lax.broadcasted_iota(jnp.int32, (rows, 128), 1) < 64


def to_rows(src_ref, sel_ref, count, put):
    nr = count * 8
    low = low_lanes(nr)
    for i in range(12):
        start = (144 * i) // 128 * 128
        width = min(256, VOX - start)
        window = src_ref[:, :, start : start + width].reshape(B * C, width)
        rows = dot_t(sel_ref[i % 8, :, :width], window)
        for e in range(2):
            for pair in range(2):
                lanes = slice(pair * 128, pair * 128 + 128)
                first = rows[2 * e * nr : (2 * e + 1) * nr, lanes]
                second = rows[(2 * e + 1) * nr : (2 * e + 2) * nr, lanes]
                put(2 * pair, i, e, jnp.where(low, first, pltpu.roll(second, 64, 1)))
                put(2 * pair + 1, i, e, jnp.where(low, pltpu.roll(first, 64, 1), second))


def from_rows(turned, sel_ref):
    total = None
    for e in range(2):
        blocks = [
            jnp.concatenate(
                [turned[(2 * e + f) * 64 : (2 * e + f + 1) * 64, ii * 128 : ii * 128 + 128] for f in range(2)], axis=1
            )
            for ii in range(6)
        ]
        part = dot(jnp.concatenate(blocks, axis=0), sel_ref[e])
        total = part if total is None else total + part
    return jnp.concatenate([total[ii * 64 : ii * 64 + 64] for ii in range(6)], axis=1)


def im2col(pad_ref, b, put, unroll=False):
    def step(ii, carry):
        for e in range(2):
            start = ii * 112 if unroll else pl.multiple_of(ii * 112, 8)
            slabs = pad_ref[b, e, pl.ds(start, 224), :]
            shifted = pltpu.roll(slabs, 223, 0)
            for a in range(3):
                for dj in range(2):
                    for dl, source in ((0, slabs), (1, shifted)):
                        pieces = []
                        for jj in range(6):
                            for s in range(2):
                                row = ((a + s) * 7 + jj + dj) * 8
                                pieces.append(source[row : row + 8])
                        put(ii, ((a * 2 + dj) * 2 + dl) * 2 + e, jnp.concatenate(pieces, axis=0).astype(BF))
        return carry

    if unroll:
        for ii in range(6):
            step(ii, 0)
    else:
        lax.fori_loop(0, 6, step, 0)


class Rounds:
    def __init__(self, pad, send_list, recv_list, z_list, bufs):
        self.pad, self.send_list, self.recv_list, self.z_list = pad, send_list, recv_list, z_list
        (self.sx, self.rx, self.sy, self.ry, self.sz, self.rz, self.ssem, self.rsem) = bufs
        self.region = lax.axis_index("region")
        self.owner = lax.axis_index("owner")

    def owner_copies(self, send, recv, base):
        out = []
        for m, t in enumerate(OFFSETS):
            out.append(
                pltpu.make_async_remote_copy(
                    src_ref=send.at[pl.ds(2 * m, 2)],
                    dst_ref=recv.at[pl.ds(2 * m, 2)],
                    send_sem=self.ssem.at[base + m],
                    recv_sem=self.rsem.at[base + m],
                    device_id=(self.region, lax.rem(self.owner + (t + N_OWNER), N_OWNER)),
                    device_id_type=MESH,
                )
            )
        return out

    def x_copies(self):
        return self.owner_copies(self.sx, self.rx, 0)

    def y_copies(self):
        return self.owner_copies(self.sy, self.ry, 4)

    def z_copies(self):
        out = []
        for m, t in enumerate((1, N_REGION - 1)):
            out.append(
                pltpu.make_async_remote_copy(
                    src_ref=self.sz.at[pl.ds(4 * m, 4)],
                    dst_ref=self.rz.at[pl.ds(4 * m, 4)],
                    send_sem=self.ssem.at[8 + m],
                    recv_sem=self.rsem.at[8 + m],
                    device_id=(lax.rem(self.region + t, N_REGION), self.owner),
                    device_id_type=MESH,
                )
            )
        return out

    def x_start(self):
        for n in range(8):
            pick = self.send_list[0, 0, n % 2, n // 2]
            slot, high = lax.rem(pick, 4), pick >= 4
            for e in range(2):
                low_face = self.pad[slot, e, 56:112, :]
                high_face = self.pad[slot, e, 672:728, :]
                self.sx[n, :, e * 128 : e * 128 + 128] = jnp.where(high, high_face, low_face).astype(BF)
        for copy in self.x_copies():
            copy.start()

    def x_end(self):
        for copy in self.x_copies():
            copy.wait_recv()
        for b in range(B):
            low_pad = self.rx[jnp.maximum(self.recv_list[0, 0, b] - 8, 0)].astype(F32)
            high_pad = self.rx[jnp.maximum(self.recv_list[0, 1, b] - 8, 0)].astype(F32)
            for e in range(2):
                self.pad[b, e, 0:56, :] = low_pad[:, e * 128 : e * 128 + 128]
                self.pad[b, e, 728:784, :] = high_pad[:, e * 128 : e * 128 + 128]

    def y_start(self):
        for n in range(8):
            pick = self.send_list[0, 1, n % 2, n // 2]
            slot, high = lax.rem(pick, 4), pick >= 4
            faces = []
            for i in range(14):
                low_face = self.pad[slot, 1, i * 56 : i * 56 + 8, :]
                high_face = self.pad[slot, 0, i * 56 + 48 : i * 56 + 56, :]
                faces.append(jnp.where(high, high_face, low_face))
            self.sy[n] = jnp.concatenate(faces, axis=0).astype(BF)
        for copy in self.y_copies():
            copy.start()

    def y_end(self):
        for copy in self.y_copies():
            copy.wait_recv()
        for b in range(B):
            low_pad = self.ry[jnp.maximum(self.recv_list[1, 0, b] - 8, 0)].astype(F32)
            high_pad = self.ry[jnp.maximum(self.recv_list[1, 1, b] - 8, 0)].astype(F32)
            for i in range(14):
                self.pad[b, 0, i * 56 : i * 56 + 8, :] = low_pad[i * 8 : i * 8 + 8]
                self.pad[b, 1, i * 56 + 48 : i * 56 + 56, :] = high_pad[i * 8 : i * 8 + 8]

    def z_start(self):
        low = low_lanes(98)
        for b in range(B):
            tiles = [self.pad[b, e, pl.ds(6, 98, stride=8), :] for e in range(2)]
            self.sz[b] = jnp.where(low, tiles[0], pltpu.roll(tiles[1], 64, 1)).astype(BF)
            tiles = [self.pad[b, e, pl.ds(0, 98, stride=8), :] for e in range(2)]
            self.sz[4 + b] = jnp.where(low, pltpu.roll(tiles[0], 64, 1), tiles[1]).astype(BF)
        for copy in self.z_copies():
            copy.start()

    def z_end(self):
        for copy in self.z_copies():
            copy.wait_recv()
        low = low_lanes(98)
        for b in range(B):
            for side in range(2):
                pick = self.z_list[side, b]
                zero = (pick == 8) | ((pick < 4) & (self.region == 0)) | ((pick >= 4) & (self.region == N_REGION - 1))
                face = self.rz[jnp.minimum(pick, 7)].astype(F32)
                face = jnp.where(zero, jnp.zeros_like(face), face)
                turned = pltpu.roll(face, 64, 1)
                row = 6 * side
                for e in range(2):
                    at = (b, e, pl.ds(row, 98, stride=8))
                    tile = self.pad[at]
                    if side == 0:
                        self.pad[at] = jnp.where(low, turned if e else face, tile)
                    else:
                        self.pad[at] = jnp.where(low, tile, face if e else turned)

    def drain(self):
        for copy in self.x_copies() + self.y_copies() + self.z_copies():
            copy.wait_send()


def round_scratch():
    return [
        pltpu.VMEM((8, 56, 256), BF),
        pltpu.VMEM((8, 56, 256), BF),
        pltpu.VMEM((8, 112, 128), BF),
        pltpu.VMEM((8, 112, 128), BF),
        pltpu.VMEM((8, 98, 128), BF),
        pltpu.VMEM((8, 98, 128), BF),
        pltpu.SemaphoreType.DMA((10,)),
        pltpu.SemaphoreType.DMA((10,)),
    ]


class Barrier:
    def __init__(self):
        self.region, self.owner = lax.axis_index("region"), lax.axis_index("owner")
        self.barrier = pltpu.get_barrier_semaphore()

    def signal(self):
        def one_owner(d, carry):
            to = (self.region, lax.rem(self.owner + d, N_OWNER))
            pl.semaphore_signal(self.barrier, inc=1, device_id=to, device_id_type=MESH)
            return carry

        def one_region(d, carry):
            to = (lax.rem(self.region + d, N_REGION), self.owner)
            pl.semaphore_signal(self.barrier, inc=1, device_id=to, device_id_type=MESH)
            return carry

        lax.fori_loop(1, N_OWNER, one_owner, 0)
        lax.fori_loop(1, N_REGION, one_region, 0)

    def wait(self):
        pl.semaphore_wait(self.barrier, N_OWNER + N_REGION - 2)


def forward_weights(weight, wide):
    zero = jnp.zeros((64, 64), BF)
    for e1 in range(2):
        for f1 in range(2):
            for k in range(TAPS):
                a, dj, dl = k // 4, k // 2 % 2, k % 2
                for e in range(2):
                    te = 2 * dj + e - e1
                    blocks = []
                    for f in range(2):
                        tf = 2 * dl + f - f1
                        ok = 0 <= te < 3 and 0 <= tf < 3
                        blocks.append(weight[9 * a + 3 * te + tf] if ok else zero)
                    row, lane = (2 * e1 + f1) * 64, k * 256 + e * 128
                    wide[row : row + 64, lane : lane + 128] = jnp.concatenate(blocks, axis=1)


def backward_weights(weight, tall):
    zero = jnp.zeros((64, 64), BF)
    for e1 in range(2):
        for k in range(TAPS):
            a, dj, dl = k // 4, k // 2 % 2, k % 2
            for e in range(2):
                te = 2 * dj + e - e1
                for f in range(2):
                    blocks = []
                    for f1 in range(2):
                        tf = 2 * dl + f - f1
                        ok = 0 <= te < 3 and 0 <= tf < 3
                        blocks.append(weight[9 * (2 - a) + 3 * (2 - te) + 2 - tf] if ok else zero)
                    row = k * 256 + (2 * e + f) * 64
                    tall[row : row + 64, e1 * 128 : e1 * 128 + 128] = jnp.concatenate(blocks, axis=1)


def pad_rows(pad, b, rows):
    low = low_lanes(48)
    edge = jnp.zeros((8, 128), F32)
    for e in range(2):
        pad[b, e, 0:56, :] = jnp.zeros((56, 128), F32)
        pad[b, e, 728:784, :] = jnp.zeros((56, 128), F32)
    for ii in range(6):
        for s in range(2):
            to = (2 * ii + s + 1) * 56
            for e in range(2):
                tile = jnp.concatenate(
                    [
                        rows[ii * 96 + jj * 16 + s * 8 : ii * 96 + jj * 16 + s * 8 + 8, e * 128 : e * 128 + 128]
                        for jj in range(6)
                    ],
                    axis=0,
                )
                tile = pltpu.roll(tile, 64, 1)
                tile = jnp.where(low, pltpu.roll(tile, 1, 0), tile)
                if e == 0:
                    pad[b, 1, to : to + 48, :] = tile
                    pad[b, 1, to + 48 : to + 56, :] = edge
                else:
                    pad[b, 0, to + 8 : to + 56, :] = tile
                    pad[b, 0, to : to + 8, :] = edge


def fold_conv(turned, cols, grads):
    low = low_lanes(64)
    main = [[None] * 3 for _ in range(3)]
    last = [[None] * 3 for _ in range(3)]

    def add(total, value):
        return value if total is None else total + value

    for a in range(3):
        for dj in range(2):
            tiles = []
            for dl in range(2):
                k = (a * 2 + dj) * 2 + dl
                total = None
                for b in range(B):
                    total = add(total, dot(turned[b], cols[b * ROWS : (b + 1) * ROWS, k * 256 : k * 256 + 256]))
                tiles.append(total)
            for e1 in range(2):
                for e in range(2):
                    te = 2 * dj + e - e1
                    if not 0 <= te < 3:
                        continue
                    lanes = slice(e * 128, e * 128 + 128)
                    t0, t1 = (tiles[dl][e1 * 128 : e1 * 128 + 64, lanes] for dl in range(2))
                    main[a][te] = add(main[a][te], t0)
                    last[a][te] = add(last[a][te], t1)
                    t0, t1 = (pltpu.roll(tiles[dl][e1 * 128 + 64 : e1 * 128 + 128, lanes], 64, 1) for dl in range(2))
                    main[a][te] = add(main[a][te], jnp.where(low, t0, t1))
                    last[a][te] = add(last[a][te], t1)
    main = main[0] + main[1] + main[2]
    last = last[0] + last[1] + last[2]

    def put(row, value):
        for start, size, part, at in split_rows(row, 64):
            grads[part, at : at + size, :] = value[start : start + size]

    for n in range(9):
        put(n * 64, main[n])
    for n in range(5):
        other = pltpu.roll(last[2 * n + 1], 64, 1) if n < 4 else jnp.zeros((64, 128), F32)
        put(576 + n * 64, jnp.where(low, last[2 * n], other))


def split_rows(row, count):
    out, start = [], 0
    while start < count:
        part, at = divmod(row + start, CHUNK)
        size = min(count - start, CHUNK - at)
        out.append((start, size, part, at))
        start += size
    return out


def step_kernel(*refs):
    inputs, (send_list, recv_list, z_list, p_send, p_recv), refs = refs[:11], refs[11:16], refs[16:]
    outputs, stage_in, stage_out, refs = refs[:5], refs[5:16], refs[16:21], refs[21:]
    feat, sel_in, weight, fgrad, sel_fg, coarse_in, down, sel_up, sel_down, eye, sel_out = stage_in
    fine, coarse, grad_in, conv_out, down_out = stage_out
    (in_sem, out_sem, pad, cols, wide, tall, mats, fg, rows8, turned, grad_turned, kids, child, grads,
     csend, crecv, dsend, drecv, first, second, mine, third, cs, cr, ds, dr, s1, r1, s2, r2, s3, r3, *bufs) = refs

    def load(n):
        return pltpu.make_async_copy(inputs[n], stage_in[n], in_sem.at[n])

    def save(n):
        return pltpu.make_async_copy(stage_out[n], outputs[n], out_sem.at[n])

    region, owner = lax.axis_index("region"), lax.axis_index("owner")
    barrier = Barrier()
    barrier.signal()
    for n in range(11):
        load(n).start()
    half = len(bufs) // 2
    ahead = Rounds(pad, send_list, recv_list, z_list, bufs[:half])
    back = Rounds(pad, send_list, recv_list, z_list, bufs[half:])

    def to_owner(src, dst, send, recv, shift):
        return pltpu.make_async_remote_copy(
            src_ref=src, dst_ref=dst, send_sem=send, recv_sem=recv,
            device_id=(region, lax.rem(owner + shift, N_OWNER)), device_id_type=MESH,
        )

    def leg1(d):
        return to_owner(grads.at[lax.rem(owner + d, N_OWNER)], first.at[d], s1.at[d], r1.at[d], d)

    def leg2(d):
        return pltpu.make_async_remote_copy(
            src_ref=second.at[region], dst_ref=second.at[region], send_sem=s2.at[d], recv_sem=r2.at[d],
            device_id=(lax.rem(region + d, N_REGION), owner), device_id_type=MESH,
        )

    def leg3(d):
        return to_owner(mine, third.at[owner], s3.at[d], r3.at[d], d)

    def each(count, leg, what):
        def body(d, carry):
            getattr(leg(d), what)()
            return carry

        lax.fori_loop(1, count, body, 0)

    def put(b, i, e, value):
        pad[b, e, (i + 1) * 56 : (i + 2) * 56, :] = value

    load(0).wait()
    load(1).wait()
    to_rows(feat, sel_in, 7, put)
    barrier.wait()
    ahead.x_start()
    kid_copies = [to_owner(csend.at[m], crecv.at[m], cs.at[m], cr.at[m], N_OWNER - m - 1) for m in range(4)]
    for n in range(2, 11):
        load(n).wait()
    for m in range(4):
        index = jnp.int32(0)
        for q in range(8):
            index = jnp.where(p_recv[0, q] == m, q, index)
        csend[m] = coarse_in[index]
        kid_copies[m].start()
    forward_weights(weight, wide)
    ahead.x_end()
    ahead.y_start()

    def put_grad(b, i, e, value):
        for jj in range(6):
            row = ((i // 2) * 6 + jj) * 16 + (i % 2) * 8
            fg[b, row : row + 8, e * 128 : e * 128 + 128] = value[jj * 8 : jj * 8 + 8]

    to_rows(fgrad, sel_fg, 6, put_grad)
    ahead.y_end()
    ahead.z_start()
    for s in range(2):
        mats[s] = jnp.concatenate([down[4 * s + n] for n in range(4)], axis=0)
    for b in range(B):
        for ii in range(6):
            rows8[b, ii * 128 + 96 : ii * 128 + 128, :] = jnp.zeros((32, 256), BF)
    for copy in kid_copies:
        copy.wait_recv()
    for k in range(B):
        index = jnp.int32(0)
        for m in range(4):
            index = jnp.where(p_send[0, m] == k, m, index)
        child[k] = crecv[index]
    backward_weights(weight, tall)
    blank = jnp.zeros((8, 128), F32)
    for b in range(B):
        up = dot(sel_up[...], child[b])
        halves = [dot_t(up.astype(BF), mats[s]) for s in range(2)]
        pieces, kid = [], []
        for t in range(36):
            cut = up[t * 8 : t * 8 + 8]
            kid += [jnp.concatenate([cut, blank], axis=1), jnp.concatenate([blank, cut], axis=1)]
            for s in range(2):
                pieces.append(halves[s][t * 8 : t * 8 + 8])
        kids[b * ROWS : (b + 1) * ROWS, :] = jnp.concatenate(kid, axis=0).astype(BF)
        fg[b] = fg[b] + jnp.concatenate(pieces, axis=0)
    ahead.z_end()

    live = lax.rem(lax.broadcasted_iota(jnp.int32, (ROWS, 256), 0), 8) < 6

    def brick(b, carry):
        base = pl.multiple_of(b * ROWS, 16)

        def put(ii, k, value):
            cols[pl.ds(pl.multiple_of(base + ii * 96, 16), 96), k * 128 : k * 128 + 128] = value

        im2col(pad, b, put)
        act = dot_t(cols[pl.ds(base, ROWS), :], wide[...])
        sig = 1.0 / (1.0 + jnp.exp(-act))
        rows = (act * sig).astype(BF)
        for ii in range(6):
            rows8[b, ii * 128 : ii * 128 + 96, :] = rows[ii * 96 : ii * 96 + 96]
        slope = sig * (1.0 + act * (1.0 - sig))
        grad = fg[b] * slope
        grad = jnp.where(live, grad, 0.0).astype(BF)
        grad_turned[b] = dot_t(eye[...], grad).astype(BF)
        pad_rows(pad, b, grad.astype(F32))
        return carry

    lax.fori_loop(0, B, brick, 0)
    back.x_start()

    for b in range(B):
        turned[b] = dot_t(eye[...], rows8[b]).astype(BF)

    fold_conv(grad_turned, cols, grads)
    total = None
    for b in range(B):
        short = jnp.concatenate([turned[b, :, ii * 128 : ii * 128 + 96] for ii in range(6)], axis=1)
        part = dot(short, kids[b * ROWS : (b + 1) * ROWS, :])
        total = part if total is None else total + part
    for s in range(2):
        for start, size, part, at in split_rows(896 + s * 256, 256):
            grads[part, at : at + size, :] = total[start : start + size, s * 128 : s * 128 + 128]
    for start, size, part, at in split_rows(1408, 128):
        grads[part, at : at + size, :] = jnp.zeros((size, 128), F32)
    each(N_OWNER, leg1, "start")
    back.x_end()
    back.y_start()

    def contribution(b, carry):
        pieces = [
            dot(jnp.concatenate([rows8[b, ii * 128 : ii * 128 + 96, :] for ii in range(6)], axis=0), mats[s])
            for s in range(2)
        ]
        sums = [pieces[0][t * 16 : t * 16 + 8] + pieces[1][t * 16 + 8 : t * 16 + 16] for t in range(36)]
        coarse_tmp = dot(sel_down[...], jnp.concatenate(sums, axis=0).astype(BF)).astype(BF)
        child[b] = coarse_tmp
        return carry

    lax.fori_loop(0, B, contribution, 0)
    up_copies = [to_owner(dsend.at[m], drecv.at[m], ds.at[m], dr.at[m], m + 1) for m in range(4)]
    for m in range(4):
        dsend[m] = child[p_send[0, m]]
        up_copies[m].start()

    back.y_end()
    back.z_start()
    for b in range(B):
        fine[b] = from_rows(turned[b], sel_out).astype(BF)
    save(0).start()
    for copy in up_copies:
        copy.wait_recv()
    drecv[4] = jnp.zeros((216, C2), BF)
    for q in range(8):
        coarse[q] = drecv[p_recv[0, q]]
    save(1).start()
    back.z_end()

    each(N_OWNER, leg1, "wait_recv")
    second[region] = lax.fori_loop(1, N_OWNER, lambda d, total: total + first[d], grads[owner])
    each(N_REGION, leg2, "start")

    def back_brick(b):
        base = b * ROWS

        def put(ii, k, value):
            cols[base + ii * 96 : base + ii * 96 + 96, k * 128 : k * 128 + 128] = value

        im2col(pad, b, put, True)
        rows = dot(cols[base : base + ROWS, :], tall[...]).astype(BF)
        for ii in range(6):
            rows8[b, ii * 128 : ii * 128 + 96, :] = rows[ii * 96 : ii * 96 + 96]

    back_brick(0)
    back_brick(1)
    each(N_REGION, leg2, "wait_recv")
    part = lax.fori_loop(1, N_REGION, lambda d, total: total + second[d], second[0])
    factor = 1.0 / math.sqrt(B * N_OWNER * N_REGION * VOX)
    part = (part * factor).astype(BF)
    mine[...] = part
    each(N_OWNER, leg3, "start")
    third[owner] = part
    back_brick(2)
    back_brick(3)
    for b in range(B):
        grad_in[b] = from_rows(dot_t(eye[...], rows8[b]).astype(BF), sel_out).astype(BF)
    save(2).start()
    each(N_OWNER, leg3, "wait_recv")
    total = third[...].astype(F32).reshape(GROWS, 128)
    for n in range(9):
        tile = total[n * 64 : n * 64 + 64]
        conv_out[3 * n] = tile[:, 0:64]
        conv_out[3 * n + 1] = tile[:, 64:128]
        row = 576 + (n // 2) * 64
        conv_out[3 * n + 2] = total[row : row + 64, (n % 2) * 64 : (n % 2) * 64 + 64]
    for t in range(8):
        down_out[t] = total[896 + t * 64 : 960 + t * 64]
    save(3).start()
    save(4).start()
    ahead.drain()
    back.drain()
    for copy in kid_copies + up_copies:
        copy.wait_send()
    each(N_OWNER, leg1, "wait_send")
    each(N_REGION, leg2, "wait_send")
    each(N_OWNER, leg3, "wait_send")
    for n in range(5):
        save(n).wait()


def tail_kernel(*refs):
    sources, results, stage, (sem_in, sem_out) = refs[:5], refs[5:10], refs[10:15], refs[15:]
    pieces = []
    for n in range(5):
        size = sources[n].shape[0]
        for k, (start, end) in enumerate(((0, size // 2), (size // 2, size))):
            at = pl.ds(start, end - start)
            pieces.append(
                (
                    pltpu.make_async_copy(sources[n].at[at], stage[n].at[at], sem_in.at[2 * n + k]),
                    pltpu.make_async_copy(stage[n].at[at], results[n].at[at], sem_out.at[2 * n + k]),
                )
            )
    for into, _ in pieces:
        into.start()
    for into, out in pieces:
        into.wait()
        out.start()
    for _, out in pieces:
        out.wait()


VM = pl.BlockSpec(memory_space=pltpu.VMEM)
ANY = pl.BlockSpec(memory_space=pl.ANY)
SM = pl.BlockSpec(memory_space=pltpu.SMEM)


def struct(shape, kind):
    return jax.ShapeDtypeStruct(shape, kind)


def local(
    features, conv_weight, down_weight, fine_grad, coarse_grad, face_send, face_recv, z_recv, parent_send, parent_recv
):
    sel_up, sel_down = coarse_selects()
    eye = np.eye(256, dtype=np.float32).astype(BF)
    big = (
        features, select_in(True), conv_weight, fine_grad, select_in(False), coarse_grad[0].transpose(1, 2, 0),
        down_weight.transpose(0, 2, 1), sel_up, sel_down, eye, select_out(),
    )
    big = tuple(jnp.asarray(x) for x in big)
    results = (
        struct((B, C, VOX), BF),
        struct((8, 216, C2), BF),
        struct((B, C, VOX), BF),
        struct((27, C, C), F32),
        struct((8, C, C2), F32),
    )
    dma = pltpu.SemaphoreType.DMA
    made = pl.pallas_call(
        step_kernel,
        out_shape=results,
        in_specs=[ANY] * 11 + [SM] * 5,
        out_specs=(ANY,) * 5,
        scratch_shapes=[pltpu.VMEM(x.shape, x.dtype) for x in big + results]
        + [dma((11,)), dma((5,))]
        + [
            pltpu.VMEM((B, 2, PROWS, 128), F32),
            pltpu.VMEM((B * ROWS, TAPS * 256), BF),
            pltpu.VMEM((256, TAPS * 256), BF),
            pltpu.VMEM((TAPS * 256, 256), BF),
            pltpu.VMEM((2, 256, C2), BF),
            pltpu.VMEM((B, ROWS, 256), F32),
            pltpu.VMEM((B, 768, 256), BF),
            pltpu.VMEM((B, 256, 768), BF),
            pltpu.VMEM((B, 256, ROWS), BF),
            pltpu.VMEM((B * ROWS, 256), BF),
            pltpu.VMEM((B, 216, C2), BF),
            pltpu.VMEM((N_OWNER, CHUNK, 128), F32),
            pltpu.VMEM((4, 216, C2), BF),
            pltpu.VMEM((4, 216, C2), BF),
            pltpu.VMEM((4, 216, C2), BF),
            pltpu.VMEM((5, 216, C2), BF),
            pltpu.VMEM((N_OWNER, CHUNK, 128), F32),
            pltpu.VMEM((N_REGION, CHUNK, 128), F32),
            pltpu.VMEM((CHUNK, 128), BF),
            pltpu.VMEM((N_OWNER, CHUNK, 128), BF),
        ]
        + [dma((4,))] * 4
        + [dma((N_OWNER,))] * 2
        + [dma((N_REGION,))] * 2
        + [dma((N_OWNER,))] * 2
        + round_scratch()
        + round_scratch(),
        compiler_params=pltpu.CompilerParams(collective_id=0, has_side_effects=True, vmem_limit_bytes=VMEM_LIMIT),
        name="step",
    )(
        *big, face_send.transpose(0, 1, 3, 2), face_recv.transpose(1, 2, 0), z_recv.transpose(1, 0), parent_send, parent_recv
    )
    fine, coarse_out, grad_in, grad_conv, grad_down = pl.pallas_call(
        tail_kernel,
        out_shape=results,
        in_specs=[ANY] * 5,
        out_specs=(ANY,) * 5,
        scratch_shapes=[pltpu.VMEM(x.shape, x.dtype) for x in results] + [dma((10,))] * 2,
        name="tail",
    )(*made)
    return fine, coarse_out.transpose(2, 0, 1)[None], grad_in, grad_conv, grad_down.transpose(0, 2, 1)


def solution(mesh):
    both = ("region", "owner")
    return jax.shard_map(
        local,
        mesh=mesh,
        in_specs=(
            P(both, None, None),
            P(),
            P(),
            P(both, None, None),
            P(both, None, None, None),
            P(both, None, None, None),
            P(both, None, None),
            P(both, None),
            P(both, None),
            P(both, None),
        ),
        out_specs=(P(both, None, None), P(both, None, None, None), P(both, None, None), P(), P()),
        check_vma=False,
    )
```

```python
import math

import jax
import jax.numpy as jnp
import numpy as np
from jax import lax
from jax.experimental import pallas as pl
from jax.experimental.pallas import tpu as pltpu
from jax.sharding import PartitionSpec as P


C = 64
C2 = 128
VOX = 1728
B = 4
PROWS = 14 * 7 * 8
ROWS = 6 * 6 * 16
TAPS = 12
OFFSETS = (1, -1, 2, -2)
N_OWNER = 32
N_REGION = 8
CHUNK = 48
GROWS = N_OWNER * CHUNK
BF = jnp.bfloat16
F32 = jnp.float32
MESH = pl.DeviceIdType.MESH
VMEM_LIMIT = 56 * 1024 * 1024


def select_in(padded):
    count = 7 if padded else 6
    back = 1 if padded else 0
    out = np.zeros((8, 4, count * 8, 256), np.float32)
    for v in range(8):
        for e in range(2):
            for f in range(2):
                for jj in range(count):
                    for ll in range(count):
                        j, l = 2 * jj + e - back, 2 * ll + f - back
                        if 0 <= j < 12 and 0 <= l < 12:
                            col = 16 * v + j * 12 + l
                            if col < 256:
                                out[v, 2 * e + f, jj * 8 + ll, col] = 1
    return out.reshape(8, 4 * count * 8, 256).astype(BF)


def select_out():
    out = np.zeros((2, 2, 128, 288), np.float32)
    for e in range(2):
        for f in range(2):
            for jj in range(6):
                for s in range(2):
                    for ll in range(6):
                        out[e, f, jj * 16 + s * 8 + ll, s * 144 + (2 * jj + e) * 12 + 2 * ll + f] = 1
    return out.reshape(2, 256, 288).astype(BF)


def coarse_selects():
    up = np.zeros((288, 216), np.float32)
    for ii in range(6):
        for jj in range(6):
            for ll in range(6):
                up[(ii * 6 + jj) * 8 + ll, ii * 36 + jj * 6 + ll] = 1
    return up.astype(BF), up.T.copy().astype(BF)


def dot(a, b):
    return jnp.dot(a, b, preferred_element_type=F32)


def dot_t(a, b):
    return lax.dot_general(a, b, (((1,), (1,)), ((), ())), preferred_element_type=F32)


def low_lanes(rows):
    return lax.broadcasted_iota(jnp.int32, (rows, 128), 1) < 64


def to_rows(src_ref, sel_ref, count, put):
    nr = count * 8
    low = low_lanes(nr)
    for i in range(12):
        start = (144 * i) // 128 * 128
        width = min(256, VOX - start)
        window = src_ref[:, :, start : start + width].reshape(B * C, width)
        rows = dot_t(sel_ref[i % 8, :, :width], window)
        for e in range(2):
            for pair in range(2):
                lanes = slice(pair * 128, pair * 128 + 128)
                first = rows[2 * e * nr : (2 * e + 1) * nr, lanes]
                second = rows[(2 * e + 1) * nr : (2 * e + 2) * nr, lanes]
                put(2 * pair, i, e, jnp.where(low, first, pltpu.roll(second, 64, 1)))
                put(2 * pair + 1, i, e, jnp.where(low, pltpu.roll(first, 64, 1), second))


def from_rows(turned, sel_ref):
    total = None
    for e in range(2):
        blocks = [
            jnp.concatenate(
                [turned[(2 * e + f) * 64 : (2 * e + f + 1) * 64, ii * 128 : ii * 128 + 128] for f in range(2)], axis=1
            )
            for ii in range(6)
        ]
        part = dot(jnp.concatenate(blocks, axis=0), sel_ref[e])
        total = part if total is None else total + part
    return jnp.concatenate([total[ii * 64 : ii * 64 + 64] for ii in range(6)], axis=1)


def im2col(pad_ref, b, put, unroll=False):
    def step(ii, carry):
        for e in range(2):
            start = ii * 112 if unroll else pl.multiple_of(ii * 112, 8)
            slabs = pad_ref[b, e, pl.ds(start, 224), :]
            shifted = pltpu.roll(slabs, 223, 0)
            for a in range(3):
                for dj in range(2):
                    for dl, source in ((0, slabs), (1, shifted)):
                        pieces = []
                        for jj in range(6):
                            for s in range(2):
                                row = ((a + s) * 7 + jj + dj) * 8
                                pieces.append(source[row : row + 8])
                        put(ii, ((a * 2 + dj) * 2 + dl) * 2 + e, jnp.concatenate(pieces, axis=0).astype(BF))
        return carry

    if unroll:
        for ii in range(6):
            step(ii, 0)
    else:
        lax.fori_loop(0, 6, step, 0)


class Rounds:
    def __init__(self, pad, send_list, recv_list, z_list, bufs):
        self.pad, self.send_list, self.recv_list, self.z_list = pad, send_list, recv_list, z_list
        (self.sx, self.rx, self.sy, self.ry, self.sz, self.rz, self.ssem, self.rsem) = bufs
        self.region = lax.axis_index("region")
        self.owner = lax.axis_index("owner")

    def owner_copies(self, send, recv, base):
        out = []
        for m, t in enumerate(OFFSETS):
            out.append(
                pltpu.make_async_remote_copy(
                    src_ref=send.at[pl.ds(2 * m, 2)],
                    dst_ref=recv.at[pl.ds(2 * m, 2)],
                    send_sem=self.ssem.at[base + m],
                    recv_sem=self.rsem.at[base + m],
                    device_id=(self.region, lax.rem(self.owner + (t + N_OWNER), N_OWNER)),
                    device_id_type=MESH,
                )
            )
        return out

    def x_copies(self):
        return self.owner_copies(self.sx, self.rx, 0)

    def y_copies(self):
        return self.owner_copies(self.sy, self.ry, 4)

    def z_copies(self):
        out = []
        for m, t in enumerate((1, N_REGION - 1)):
            out.append(
                pltpu.make_async_remote_copy(
                    src_ref=self.sz.at[pl.ds(4 * m, 4)],
                    dst_ref=self.rz.at[pl.ds(4 * m, 4)],
                    send_sem=self.ssem.at[8 + m],
                    recv_sem=self.rsem.at[8 + m],
                    device_id=(lax.rem(self.region + t, N_REGION), self.owner),
                    device_id_type=MESH,
                )
            )
        return out

    def x_start(self):
        for n in range(8):
            pick = self.send_list[0, 0, n % 2, n // 2]
            slot, high = lax.rem(pick, 4), pick >= 4
            for e in range(2):
                low_face = self.pad[slot, e, 56:112, :]
                high_face = self.pad[slot, e, 672:728, :]
                self.sx[n, :, e * 128 : e * 128 + 128] = jnp.where(high, high_face, low_face).astype(BF)
        for copy in self.x_copies():
            copy.start()

    def x_end(self):
        for copy in self.x_copies():
            copy.wait_recv()
        for b in range(B):
            low_pad = self.rx[jnp.maximum(self.recv_list[0, 0, b] - 8, 0)].astype(F32)
            high_pad = self.rx[jnp.maximum(self.recv_list[0, 1, b] - 8, 0)].astype(F32)
            for e in range(2):
                self.pad[b, e, 0:56, :] = low_pad[:, e * 128 : e * 128 + 128]
                self.pad[b, e, 728:784, :] = high_pad[:, e * 128 : e * 128 + 128]

    def y_start(self):
        for n in range(8):
            pick = self.send_list[0, 1, n % 2, n // 2]
            slot, high = lax.rem(pick, 4), pick >= 4
            faces = []
            for i in range(14):
                low_face = self.pad[slot, 1, i * 56 : i * 56 + 8, :]
                high_face = self.pad[slot, 0, i * 56 + 48 : i * 56 + 56, :]
                faces.append(jnp.where(high, high_face, low_face))
            self.sy[n] = jnp.concatenate(faces, axis=0).astype(BF)
        for copy in self.y_copies():
            copy.start()

    def y_end(self):
        for copy in self.y_copies():
            copy.wait_recv()
        for b in range(B):
            low_pad = self.ry[jnp.maximum(self.recv_list[1, 0, b] - 8, 0)].astype(F32)
            high_pad = self.ry[jnp.maximum(self.recv_list[1, 1, b] - 8, 0)].astype(F32)
            for i in range(14):
                self.pad[b, 0, i * 56 : i * 56 + 8, :] = low_pad[i * 8 : i * 8 + 8]
                self.pad[b, 1, i * 56 + 48 : i * 56 + 56, :] = high_pad[i * 8 : i * 8 + 8]

    def z_start(self):
        low = low_lanes(98)
        for b in range(B):
            tiles = [self.pad[b, e, pl.ds(6, 98, stride=8), :] for e in range(2)]
            self.sz[b] = jnp.where(low, tiles[0], pltpu.roll(tiles[1], 64, 1)).astype(BF)
            tiles = [self.pad[b, e, pl.ds(0, 98, stride=8), :] for e in range(2)]
            self.sz[4 + b] = jnp.where(low, pltpu.roll(tiles[0], 64, 1), tiles[1]).astype(BF)
        for copy in self.z_copies():
            copy.start()

    def z_end(self):
        for copy in self.z_copies():
            copy.wait_recv()
        low = low_lanes(98)
        for b in range(B):
            for side in range(2):
                pick = self.z_list[side, b]
                zero = (pick == 8) | ((pick < 4) & (self.region == 0)) | ((pick >= 4) & (self.region == N_REGION - 1))
                face = self.rz[jnp.minimum(pick, 7)].astype(F32)
                face = jnp.where(zero, jnp.zeros_like(face), face)
                turned = pltpu.roll(face, 64, 1)
                row = 6 * side
                for e in range(2):
                    at = (b, e, pl.ds(row, 98, stride=8))
                    tile = self.pad[at]
                    if side == 0:
                        self.pad[at] = jnp.where(low, turned if e else face, tile)
                    else:
                        self.pad[at] = jnp.where(low, tile, face if e else turned)

    def drain(self):
        for copy in self.x_copies() + self.y_copies() + self.z_copies():
            copy.wait_send()


def round_scratch():
    return [
        pltpu.VMEM((8, 56, 256), BF),
        pltpu.VMEM((8, 56, 256), BF),
        pltpu.VMEM((8, 112, 128), BF),
        pltpu.VMEM((8, 112, 128), BF),
        pltpu.VMEM((8, 98, 128), BF),
        pltpu.VMEM((8, 98, 128), BF),
        pltpu.SemaphoreType.DMA((10,)),
        pltpu.SemaphoreType.DMA((10,)),
    ]


class Barrier:
    def __init__(self):
        self.region, self.owner = lax.axis_index("region"), lax.axis_index("owner")
        self.barrier = pltpu.get_barrier_semaphore()

    def signal(self):
        def one_owner(d, carry):
            to = (self.region, lax.rem(self.owner + d, N_OWNER))
            pl.semaphore_signal(self.barrier, inc=1, device_id=to, device_id_type=MESH)
            return carry

        def one_region(d, carry):
            to = (lax.rem(self.region + d, N_REGION), self.owner)
            pl.semaphore_signal(self.barrier, inc=1, device_id=to, device_id_type=MESH)
            return carry

        lax.fori_loop(1, N_OWNER, one_owner, 0)
        lax.fori_loop(1, N_REGION, one_region, 0)

    def wait(self):
        pl.semaphore_wait(self.barrier, N_OWNER + N_REGION - 2)


def forward_weights(weight, wide):
    zero = jnp.zeros((64, 64), BF)
    for e1 in range(2):
        for f1 in range(2):
            for k in range(TAPS):
                a, dj, dl = k // 4, k // 2 % 2, k % 2
                for e in range(2):
                    te = 2 * dj + e - e1
                    blocks = []
                    for f in range(2):
                        tf = 2 * dl + f - f1
                        ok = 0 <= te < 3 and 0 <= tf < 3
                        blocks.append(weight[9 * a + 3 * te + tf] if ok else zero)
                    row, lane = (2 * e1 + f1) * 64, k * 256 + e * 128
                    wide[row : row + 64, lane : lane + 128] = jnp.concatenate(blocks, axis=1)


def backward_weights(weight, tall):
    zero = jnp.zeros((64, 64), BF)
    for e1 in range(2):
        for k in range(TAPS):
            a, dj, dl = k // 4, k // 2 % 2, k % 2
            for e in range(2):
                te = 2 * dj + e - e1
                for f in range(2):
                    blocks = []
                    for f1 in range(2):
                        tf = 2 * dl + f - f1
                        ok = 0 <= te < 3 and 0 <= tf < 3
                        blocks.append(weight[9 * (2 - a) + 3 * (2 - te) + 2 - tf] if ok else zero)
                    row = k * 256 + (2 * e + f) * 64
                    tall[row : row + 64, e1 * 128 : e1 * 128 + 128] = jnp.concatenate(blocks, axis=1)


def pad_rows(pad, b, rows):
    low = low_lanes(48)
    edge = jnp.zeros((8, 128), F32)
    for e in range(2):
        pad[b, e, 0:56, :] = jnp.zeros((56, 128), F32)
        pad[b, e, 728:784, :] = jnp.zeros((56, 128), F32)
    for ii in range(6):
        for s in range(2):
            to = (2 * ii + s + 1) * 56
            for e in range(2):
                tile = jnp.concatenate(
                    [
                        rows[ii * 96 + jj * 16 + s * 8 : ii * 96 + jj * 16 + s * 8 + 8, e * 128 : e * 128 + 128]
                        for jj in range(6)
                    ],
                    axis=0,
                )
                tile = pltpu.roll(tile, 64, 1)
                tile = jnp.where(low, pltpu.roll(tile, 1, 0), tile)
                if e == 0:
                    pad[b, 1, to : to + 48, :] = tile
                    pad[b, 1, to + 48 : to + 56, :] = edge
                else:
                    pad[b, 0, to + 8 : to + 56, :] = tile
                    pad[b, 0, to : to + 8, :] = edge


def fold_conv(turned, cols, grads):
    low = low_lanes(64)
    main = [[None] * 3 for _ in range(3)]
    last = [[None] * 3 for _ in range(3)]

    def add(total, value):
        return value if total is None else total + value

    for a in range(3):
        for dj in range(2):
            tiles = []
            for dl in range(2):
                k = (a * 2 + dj) * 2 + dl
                total = None
                for b in range(B):
                    total = add(total, dot(turned[b], cols[b * ROWS : (b + 1) * ROWS, k * 256 : k * 256 + 256]))
                tiles.append(total)
            for e1 in range(2):
                for e in range(2):
                    te = 2 * dj + e - e1
                    if not 0 <= te < 3:
                        continue
                    lanes = slice(e * 128, e * 128 + 128)
                    t0, t1 = (tiles[dl][e1 * 128 : e1 * 128 + 64, lanes] for dl in range(2))
                    main[a][te] = add(main[a][te], t0)
                    last[a][te] = add(last[a][te], t1)
                    t0, t1 = (pltpu.roll(tiles[dl][e1 * 128 + 64 : e1 * 128 + 128, lanes], 64, 1) for dl in range(2))
                    main[a][te] = add(main[a][te], jnp.where(low, t0, t1))
                    last[a][te] = add(last[a][te], t1)
    main = main[0] + main[1] + main[2]
    last = last[0] + last[1] + last[2]

    def put(row, value):
        for start, size, part, at in split_rows(row, 64):
            grads[part, at : at + size, :] = value[start : start + size].astype(BF)

    for n in range(9):
        put(n * 64, main[n])
    for n in range(5):
        other = pltpu.roll(last[2 * n + 1], 64, 1) if n < 4 else jnp.zeros((64, 128), F32)
        put(576 + n * 64, jnp.where(low, last[2 * n], other))


def split_rows(row, count):
    out, start = [], 0
    while start < count:
        part, at = divmod(row + start, CHUNK)
        size = min(count - start, CHUNK - at)
        out.append((start, size, part, at))
        start += size
    return out


def step_kernel(*refs):
    inputs, (send_list, recv_list, z_list, p_send, p_recv), refs = refs[:11], refs[11:16], refs[16:]
    outputs, stage_in, stage_out, refs = refs[:5], refs[5:16], refs[16:21], refs[21:]
    feat, sel_in, weight, fgrad, sel_fg, coarse_in, down, sel_up, sel_down, eye, sel_out = stage_in
    fine, coarse, grad_in, conv_out, down_out = stage_out
    (in_sem, out_sem, pad, cols, wide, tall, mats, fg, rows8, turned, grad_turned, kids, child, grads,
     csend, crecv, dsend, drecv, first, second, mine, third, cs, cr, ds, dr, s1, r1, s2, r2, s3, r3, *bufs) = refs

    def load(n):
        return pltpu.make_async_copy(inputs[n], stage_in[n], in_sem.at[n])

    def save(n):
        return pltpu.make_async_copy(stage_out[n], outputs[n], out_sem.at[n])

    region, owner = lax.axis_index("region"), lax.axis_index("owner")
    barrier = Barrier()
    barrier.signal()
    for n in range(11):
        load(n).start()
    half = len(bufs) // 2
    ahead = Rounds(pad, send_list, recv_list, z_list, bufs[:half])
    back = Rounds(pad, send_list, recv_list, z_list, bufs[half:])

    def to_owner(src, dst, send, recv, shift):
        return pltpu.make_async_remote_copy(
            src_ref=src, dst_ref=dst, send_sem=send, recv_sem=recv,
            device_id=(region, lax.rem(owner + shift, N_OWNER)), device_id_type=MESH,
        )

    def leg1(d):
        return to_owner(grads.at[lax.rem(owner + d, N_OWNER)], first.at[d], s1.at[d], r1.at[d], d)

    def leg2(d):
        return pltpu.make_async_remote_copy(
            src_ref=second.at[region], dst_ref=second.at[region], send_sem=s2.at[d], recv_sem=r2.at[d],
            device_id=(lax.rem(region + d, N_REGION), owner), device_id_type=MESH,
        )

    def leg3(d):
        return to_owner(mine, third.at[owner], s3.at[d], r3.at[d], d)

    def each(count, leg, what):
        def body(d, carry):
            getattr(leg(d), what)()
            return carry

        lax.fori_loop(1, count, body, 0)

    def put(b, i, e, value):
        pad[b, e, (i + 1) * 56 : (i + 2) * 56, :] = value

    load(0).wait()
    load(1).wait()
    to_rows(feat, sel_in, 7, put)
    barrier.wait()
    ahead.x_start()
    kid_copies = [to_owner(csend.at[m], crecv.at[m], cs.at[m], cr.at[m], N_OWNER - m - 1) for m in range(4)]
    for n in range(2, 11):
        load(n).wait()
    for m in range(4):
        index = jnp.int32(0)
        for q in range(8):
            index = jnp.where(p_recv[0, q] == m, q, index)
        csend[m] = coarse_in[index]
        kid_copies[m].start()
    forward_weights(weight, wide)
    ahead.x_end()
    ahead.y_start()

    def put_grad(b, i, e, value):
        for jj in range(6):
            row = ((i // 2) * 6 + jj) * 16 + (i % 2) * 8
            fg[b, row : row + 8, e * 128 : e * 128 + 128] = value[jj * 8 : jj * 8 + 8]

    to_rows(fgrad, sel_fg, 6, put_grad)
    ahead.y_end()
    ahead.z_start()
    for s in range(2):
        mats[s] = jnp.concatenate([down[4 * s + n] for n in range(4)], axis=0)
    for b in range(B):
        for ii in range(6):
            rows8[b, ii * 128 + 96 : ii * 128 + 128, :] = jnp.zeros((32, 256), BF)
    for copy in kid_copies:
        copy.wait_recv()
    for k in range(B):
        index = jnp.int32(0)
        for m in range(4):
            index = jnp.where(p_send[0, m] == k, m, index)
        child[k] = crecv[index]
    backward_weights(weight, tall)
    blank = jnp.zeros((8, 128), F32)
    for b in range(B):
        up = dot(sel_up[...], child[b])
        halves = [dot_t(up.astype(BF), mats[s]) for s in range(2)]
        pieces, kid = [], []
        for t in range(36):
            cut = up[t * 8 : t * 8 + 8]
            kid += [jnp.concatenate([cut, blank], axis=1), jnp.concatenate([blank, cut], axis=1)]
            for s in range(2):
                pieces.append(halves[s][t * 8 : t * 8 + 8])
        kids[b * ROWS : (b + 1) * ROWS, :] = jnp.concatenate(kid, axis=0).astype(BF)
        fg[b] = fg[b] + jnp.concatenate(pieces, axis=0)
    ahead.z_end()

    live = lax.rem(lax.broadcasted_iota(jnp.int32, (ROWS, 256), 0), 8) < 6

    def brick(b, carry):
        base = pl.multiple_of(b * ROWS, 16)

        def put(ii, k, value):
            cols[pl.ds(pl.multiple_of(base + ii * 96, 16), 96), k * 128 : k * 128 + 128] = value

        im2col(pad, b, put)
        act = dot_t(cols[pl.ds(base, ROWS), :], wide[...])
        sig = 1.0 / (1.0 + jnp.exp(-act))
        rows = (act * sig).astype(BF)
        for ii in range(6):
            rows8[b, ii * 128 : ii * 128 + 96, :] = rows[ii * 96 : ii * 96 + 96]
        slope = sig * (1.0 + act * (1.0 - sig))
        grad = fg[b] * slope
        grad = jnp.where(live, grad, 0.0).astype(BF)
        grad_turned[b] = dot_t(eye[...], grad).astype(BF)
        pad_rows(pad, b, grad.astype(F32))
        return carry

    lax.fori_loop(0, B, brick, 0)
    back.x_start()

    for b in range(B):
        turned[b] = dot_t(eye[...], rows8[b]).astype(BF)

    total = None
    for b in range(B):
        short = jnp.concatenate([turned[b, :, ii * 128 : ii * 128 + 96] for ii in range(6)], axis=1)
        part = dot(short, kids[b * ROWS : (b + 1) * ROWS, :])
        total = part if total is None else total + part
    for s in range(2):
        for start, size, part, at in split_rows(896 + s * 256, 256):
            grads[part, at : at + size, :] = total[start : start + size, s * 128 : s * 128 + 128].astype(BF)
    for start, size, part, at in split_rows(1408, 128):
        grads[part, at : at + size, :] = jnp.zeros((size, 128), BF)
    def send_parts(late):
        def body(d, carry):
            here = lax.rem(owner + d, N_OWNER) <= 896 // CHUNK

            @pl.when(here if late else jnp.logical_not(here))
            def _():
                leg1(d).start()

            return carry

        lax.fori_loop(1, N_OWNER, body, 0)

    send_parts(False)
    fold_conv(grad_turned, cols, grads)
    back.x_end()
    back.y_start()

    def contribution(b, carry):
        pieces = [
            dot(jnp.concatenate([rows8[b, ii * 128 : ii * 128 + 96, :] for ii in range(6)], axis=0), mats[s])
            for s in range(2)
        ]
        sums = [pieces[0][t * 16 : t * 16 + 8] + pieces[1][t * 16 + 8 : t * 16 + 16] for t in range(36)]
        coarse_tmp = dot(sel_down[...], jnp.concatenate(sums, axis=0).astype(BF)).astype(BF)
        child[b] = coarse_tmp
        return carry

    lax.fori_loop(0, B, contribution, 0)
    up_copies = [to_owner(dsend.at[m], drecv.at[m], ds.at[m], dr.at[m], m + 1) for m in range(4)]
    for m in range(4):
        dsend[m] = child[p_send[0, m]]
        up_copies[m].start()

    back.y_end()
    back.z_start()
    send_parts(True)
    for b in range(B):
        fine[b] = from_rows(turned[b], sel_out).astype(BF)
    save(0).start()
    for copy in up_copies:
        copy.wait_recv()
    drecv[4] = jnp.zeros((216, C2), BF)
    for q in range(8):
        coarse[q] = drecv[p_recv[0, q]]
    save(1).start()
    back.z_end()

    each(N_OWNER, leg1, "wait_recv")
    part = grads[owner].astype(F32)
    for d in range(1, N_OWNER):
        part = part + first[d].astype(F32)
    second[region] = part.astype(BF)
    each(N_REGION, leg2, "start")

    def back_brick(b):
        base = b * ROWS

        def put(ii, k, value):
            cols[base + ii * 96 : base + ii * 96 + 96, k * 128 : k * 128 + 128] = value

        im2col(pad, b, put, True)
        rows = dot(cols[base : base + ROWS, :], tall[...]).astype(BF)
        for ii in range(6):
            rows8[b, ii * 128 : ii * 128 + 96, :] = rows[ii * 96 : ii * 96 + 96]

    back_brick(0)
    back_brick(1)
    each(N_REGION, leg2, "wait_recv")
    part = second[0].astype(F32)
    for d in range(1, N_REGION):
        part = part + second[d].astype(F32)
    factor = 1.0 / math.sqrt(B * N_OWNER * N_REGION * VOX)
    part = (part * factor).astype(BF)
    mine[...] = part
    each(N_OWNER, leg3, "start")
    third[owner] = part
    back_brick(2)
    back_brick(3)
    for b in range(B):
        grad_in[b] = from_rows(dot_t(eye[...], rows8[b]).astype(BF), sel_out).astype(BF)
    save(2).start()
    each(N_OWNER, leg3, "wait_recv")
    total = third[...].astype(F32).reshape(GROWS, 128)
    for n in range(9):
        tile = total[n * 64 : n * 64 + 64]
        conv_out[3 * n] = tile[:, 0:64]
        conv_out[3 * n + 1] = tile[:, 64:128]
        row = 576 + (n // 2) * 64
        conv_out[3 * n + 2] = total[row : row + 64, (n % 2) * 64 : (n % 2) * 64 + 64]
    for t in range(8):
        down_out[t] = total[896 + t * 64 : 960 + t * 64]
    save(3).start()
    save(4).start()
    ahead.drain()
    back.drain()
    for copy in kid_copies + up_copies:
        copy.wait_send()
    each(N_OWNER, leg1, "wait_send")
    each(N_REGION, leg2, "wait_send")
    each(N_OWNER, leg3, "wait_send")
    for n in range(5):
        save(n).wait()


def tail_kernel(*refs):
    sources, results, stage, (sem_in, sem_out) = refs[:5], refs[5:10], refs[10:15], refs[15:]
    pieces = []
    for n in range(5):
        size = sources[n].shape[0]
        for k, (start, end) in enumerate(((0, size // 2), (size // 2, size))):
            at = pl.ds(start, end - start)
            pieces.append(
                (
                    pltpu.make_async_copy(sources[n].at[at], stage[n].at[at], sem_in.at[2 * n + k]),
                    pltpu.make_async_copy(stage[n].at[at], results[n].at[at], sem_out.at[2 * n + k]),
                )
            )
    for into, _ in pieces:
        into.start()
    for into, out in pieces:
        into.wait()
        out.start()
    for _, out in pieces:
        out.wait()


VM = pl.BlockSpec(memory_space=pltpu.VMEM)
ANY = pl.BlockSpec(memory_space=pl.ANY)
SM = pl.BlockSpec(memory_space=pltpu.SMEM)


def struct(shape, kind):
    return jax.ShapeDtypeStruct(shape, kind)


def local(
    features, conv_weight, down_weight, fine_grad, coarse_grad, face_send, face_recv, z_recv, parent_send, parent_recv
):
    sel_up, sel_down = coarse_selects()
    eye = np.eye(256, dtype=np.float32).astype(BF)
    big = (
        features, select_in(True), conv_weight, fine_grad, select_in(False), coarse_grad[0].transpose(1, 2, 0),
        down_weight.transpose(0, 2, 1), sel_up, sel_down, eye, select_out(),
    )
    big = tuple(jnp.asarray(x) for x in big)
    results = (
        struct((B, C, VOX), BF),
        struct((8, 216, C2), BF),
        struct((B, C, VOX), BF),
        struct((27, C, C), F32),
        struct((8, C, C2), F32),
    )
    dma = pltpu.SemaphoreType.DMA
    made = pl.pallas_call(
        step_kernel,
        out_shape=results,
        in_specs=[ANY] * 11 + [SM] * 5,
        out_specs=(ANY,) * 5,
        scratch_shapes=[pltpu.VMEM(x.shape, x.dtype) for x in big + results]
        + [dma((11,)), dma((5,))]
        + [
            pltpu.VMEM((B, 2, PROWS, 128), F32),
            pltpu.VMEM((B * ROWS, TAPS * 256), BF),
            pltpu.VMEM((256, TAPS * 256), BF),
            pltpu.VMEM((TAPS * 256, 256), BF),
            pltpu.VMEM((2, 256, C2), BF),
            pltpu.VMEM((B, ROWS, 256), F32),
            pltpu.VMEM((B, 768, 256), BF),
            pltpu.VMEM((B, 256, 768), BF),
            pltpu.VMEM((B, 256, ROWS), BF),
            pltpu.VMEM((B * ROWS, 256), BF),
            pltpu.VMEM((B, 216, C2), BF),
            pltpu.VMEM((N_OWNER, CHUNK, 128), BF),
            pltpu.VMEM((4, 216, C2), BF),
            pltpu.VMEM((4, 216, C2), BF),
            pltpu.VMEM((4, 216, C2), BF),
            pltpu.VMEM((5, 216, C2), BF),
            pltpu.VMEM((N_OWNER, CHUNK, 128), BF),
            pltpu.VMEM((N_REGION, CHUNK, 128), BF),
            pltpu.VMEM((CHUNK, 128), BF),
            pltpu.VMEM((N_OWNER, CHUNK, 128), BF),
        ]
        + [dma((4,))] * 4
        + [dma((N_OWNER,))] * 2
        + [dma((N_REGION,))] * 2
        + [dma((N_OWNER,))] * 2
        + round_scratch()
        + round_scratch(),
        compiler_params=pltpu.CompilerParams(collective_id=0, has_side_effects=True, vmem_limit_bytes=VMEM_LIMIT),
        name="step",
    )(
        *big, face_send.transpose(0, 1, 3, 2), face_recv.transpose(1, 2, 0), z_recv.transpose(1, 0), parent_send, parent_recv
    )
    fine, coarse_out, grad_in, grad_conv, grad_down = pl.pallas_call(
        tail_kernel,
        out_shape=results,
        in_specs=[ANY] * 5,
        out_specs=(ANY,) * 5,
        scratch_shapes=[pltpu.VMEM(x.shape, x.dtype) for x in results] + [dma((10,))] * 2,
        name="tail",
    )(*made)
    return fine, coarse_out.transpose(2, 0, 1)[None], grad_in, grad_conv, grad_down.transpose(0, 2, 1)


def solution(mesh):
    both = ("region", "owner")
    return jax.shard_map(
        local,
        mesh=mesh,
        in_specs=(
            P(both, None, None),
            P(),
            P(),
            P(both, None, None),
            P(both, None, None, None),
            P(both, None, None, None),
            P(both, None, None),
            P(both, None),
            P(both, None),
            P(both, None),
        ),
        out_specs=(P(both, None, None), P(both, None, None, None), P(both, None, None), P(), P()),
        check_vma=False,
    )
```
